128 devices in a mesh: batch: 8 (over x, core), item: 16 (over y, z).
Axes of the slice: x: 4, y: 4, z: 4, core: 2. Of those that a mesh axis runs over, the one named last changes fastest.
Arguments:
- item_table: bfloat16 [32768, 256], P('item'), may hold values from -6 to 6
- neighbours: int32 [256, 32], P('item', 'batch'), may hold values from 0 to 255, as said below
- tile_weights: bfloat16 [256, 32, 128, 128], P('item', 'batch'), may hold values from -0.09375 to 0.09375
- history: int32 [2048, 256], P(('batch', 'item')), may hold values from 0 to 32767, as said below
- lengths: int32 [2048], P(('batch', 'item')), may hold values from 1 to 256, 262144 in all
- position: float32 [256, 256], replicated, may hold values from -3 to 3
- norm_gain: float32 [256], replicated, may hold values from 0.1 to 1.9
- in_weight: bfloat16 [256, 768], replicated, may hold values from -2 to 2
- out_weight: bfloat16 [256, 256], replicated, may hold values from -0.375 to 0.375
- cotangent: bfloat16 [2048, 256, 256], P(('batch', 'item')), may hold values from -0.032958984 to 0.032958984
Outputs:
- block_out: bfloat16 [2048, 256, 256], P(('batch', 'item'))
- grad_in_weight: float32 [256, 768], replicated
- grad_out_weight: float32 [256, 256], replicated
- grad_norm_gain: float32 [256], replicated
- grad_position: float32 [256, 256], replicated
The draws below stay inside these ranges and needn't reach their ends.
Inputs may be any that keep to these rules, and one draw needn't show every extreme that they name: `neighbours`: row tile t lies on item shard s = t // 16; its slots name only tiles of shards s - 1, s and s + 1, taken cyclically over the shards; a tile may repeat among the slots. `history`: item ids fall into runs of 256 consecutive ids, run r holding ids r * 256 to (r + 1) * 256 - 1. The 4096 ids of each aligned block of 16 users (all positions, live or not) name every run exactly 32 times.
All inputs are finite; a program needn't handle non-finite values. No bound on the sum of `lengths` on one device may be relied on, other than what follows from the above.
Results may differ from the reference program's by a relative error of at most 0.029.
The reference program's roundings to bfloat16 on the way count: a program that leaves them out, or rounds other values in their place, can miss the bound.
Values may be sent and summed in bfloat16 or wider, within the bound.
No kernel may reach another device: no remote copies, remote signals or barrier semaphores. Data moves between devices by JAX's collectives and lax.ppermute only.
A program may use at most 64 MiB of HBM per device.

```python
import math
import jax
import jax.numpy as jnp
import numpy as np
from jax import lax

D = 256
HEADS = 8
TILE = 128
L = 256
U_DEV = 16
ITEMS = 32768
TILES_DEV = 16
NTILES = 256
NBR = 32
ROWS_OWN = 256
USERS = 2048
TOK_DEV = 4096
CAP = 32


def draw_neighbours(key, part):
    tile_index = jnp.arange(NTILES, dtype=jnp.int32)
    shard_index = tile_index // TILES_DEV
    picked = jax.random.randint(jax.random.fold_in(key, 21), (NTILES, NBR), 0, 3 * TILES_DEV, dtype=jnp.int32)
    return jnp.mod((shard_index[:, None] - 1) * TILES_DEV + picked, NTILES).astype(jnp.int32)


def draw_history(key, part):
    block_count = USERS // U_DEV
    block_keys = jax.random.split(jax.random.fold_in(key, 11), block_count)
    shuffled = jax.vmap(lambda one_key: jax.random.permutation(one_key, TOK_DEV))(block_keys)
    run_index = (shuffled // CAP).astype(jnp.int32)
    offsets = jax.random.randint(jax.random.fold_in(key, 12), (block_count, TOK_DEV), 0, ROWS_OWN, dtype=jnp.int32)
    return (run_index * ROWS_OWN + offsets).astype(jnp.int32).reshape(USERS, L)


def draw_in_weight(key, part):
    base_key = jax.random.fold_in(key, 31)
    raw_values = jnp.clip(jax.random.normal(base_key, (D, 3 * D), jnp.float32), -4.0, 4.0) * D ** (-0.5)
    return raw_values.astype(jnp.bfloat16)


def block_scale(own_key, dims, shards, least, largest):
    def one(dim, shards_of):
        steps = jax.random.uniform(jax.random.fold_in(jax.random.fold_in(own_key, 6), dim), (shards_of,), jnp.float32, least / len(shards), largest / len(shards))
        return jnp.repeat(jnp.exp(steps), dims[dim] // shards_of).reshape((-1,) + (1,) * (len(dims) - dim - 1))

    gain = one(*shards[0])
    for cut in shards[1:]:
        gain = gain * one(*cut)
    return gain


def split_up(amount, total, bound, skew):
    portions = [(1 << 20) // math.isqrt(rank ** skew) + 1 for rank in range(2, amount + 1)]
    spare, counts = total - bound - (amount - 1), [1] * (amount - 1)
    while spare > 0:
        movable = [i for i in range(amount - 1) if counts[i] < bound]
        whole, left = sum([portions[i] for i in movable]), spare
        for i in movable:
            more = min(bound - counts[i], max(1, left * portions[i] // whole), spare)
            counts[i] = counts[i] + more
            spare = spare - more
    return np.array([bound] + counts)


def uneven(key, count, total, bound, lean):
    if count == 2:
        one = jax.random.randint(key, (), max(1, total - bound), min(bound, total - 1) + 1)
        return jnp.stack([one, total - one])
    sizes = jnp.asarray(split_up(count, total, bound, lean), jnp.int32)
    twos = (count - 1) // 2
    source_of, taker = sizes[1:1 + 2 * twos:2], sizes[2:2 + 2 * twos:2]
    margin = jnp.minimum(source_of - 1, bound - taker)
    shifted = jax.random.randint(jax.random.fold_in(key, 1), (twos,), 0, 1 << 20) % (margin + 1)
    sizes = sizes.at[1:1 + 2 * twos:2].set(source_of - shifted).at[2:2 + 2 * twos:2].set(taker + shifted)
    return sizes[jax.random.permutation(jax.random.fold_in(key, 2), count)]


def bell_draw(own_key, dims, spread, bound, shards=(), held_as=jnp.bfloat16):
    result = jax.random.normal(own_key, dims, jnp.float32) * spread
    if len(shards) > 0:
        result = block_scale(own_key, dims, shards, -0.22, 0.18) * result
    return jnp.clip(result, min=-bound, max=bound).astype(held_as)


def setup_inputs(seed: int = 0) -> dict:
    arg_keys = jax.random.split(jax.random.key(seed), 11)
    item_table = bell_draw(arg_keys[0], (ITEMS, D), 1.0, 6.0, ((0, 16),))
    neighbours = draw_neighbours(jax.random.fold_in(arg_keys[10], 71), 0)
    tile_weights = bell_draw(arg_keys[2], (NTILES, NBR, TILE, TILE), (NBR * TILE) ** -0.5, 0.09375, ((0, 16), (1, 8)))
    history = draw_history(jax.random.fold_in(arg_keys[10], 71), 0)
    lengths = uneven(arg_keys[4], USERS, USERS * L // 2, L, 2).astype(jnp.int32)
    position = bell_draw(arg_keys[5], (L, D), 0.5, 3.0, (), jnp.float32)
    norm_gain = jnp.clip(1.0 + 0.18 * jax.random.normal(arg_keys[6], (D,), jnp.float32), 0.1, 1.9)
    in_weight = draw_in_weight(jax.random.fold_in(arg_keys[10], 71), 0)
    out_weight = bell_draw(arg_keys[8], (D, D), D ** -0.5, 0.375)
    cotangent = bell_draw(arg_keys[9], (USERS, L, D), (1.0 / (USERS * 16) ** 0.5), 0.032958984, ((0, 128),))
    return dict(item_table=item_table, neighbours=neighbours, tile_weights=tile_weights, history=history, lengths=lengths, position=position, norm_gain=norm_gain, in_weight=in_weight, out_weight=out_weight, cotangent=cotangent)


def block_pass(rows_in, lens, cot_rows, position, norm_gain, in_weight, out_weight):
    group_size, length, feat_width = rows_in.shape
    head_dim = feat_width // HEADS
    score_scale = head_dim ** (-0.5)
    flat_count = group_size * length
    residual = rows_in.astype(jnp.float32) + position
    inv_rms = lax.rsqrt(lax.optimization_barrier(jnp.mean(residual * residual, axis=-1, keepdims=True)) + 1e-05)
    normed = (residual * inv_rms * norm_gain).astype(jnp.bfloat16)
    flat_normed = normed.reshape(flat_count, feat_width)
    qkv = jnp.dot(flat_normed, in_weight, preferred_element_type=jnp.float32).astype(jnp.bfloat16)
    query_rows = qkv[:, :feat_width].reshape(group_size, length, HEADS, head_dim)
    key_rows = qkv[:, feat_width:2 * feat_width].reshape(group_size, length, HEADS, head_dim)
    value_rows = qkv[:, 2 * feat_width:].reshape(group_size, length, HEADS, head_dim)
    scores = jnp.einsum('gihe,gjhe->ghij', query_rows.astype(jnp.float32), key_rows.astype(jnp.float32)) * score_scale
    places = jnp.arange(length)
    allowed = (places[None, :] <= places[:, None])[None, None] & (places[None, None, None, :] < lens[:, None, None, None])
    scores = jnp.where(allowed, scores, -1e+30)
    row_top = lax.optimization_barrier(jnp.max(scores, axis=-1, keepdims=True))
    weights_exp = jnp.where(allowed, jnp.exp(scores - row_top), 0.0)
    prob_full = weights_exp / lax.optimization_barrier(jnp.sum(weights_exp, axis=-1, keepdims=True))
    probs_low = prob_full.astype(jnp.bfloat16)
    mixed_rows = jnp.einsum('ghij,gjhe->gihe', probs_low.astype(jnp.float32), value_rows.astype(jnp.float32))
    mixed_rows = mixed_rows.astype(jnp.bfloat16).reshape(flat_count, feat_width)
    attn_rows = jnp.dot(mixed_rows, out_weight, preferred_element_type=jnp.float32)
    live_mask = (places[None, :] < lens[:, None]).astype(jnp.float32).reshape(flat_count, 1)
    flat_resid = residual.reshape(flat_count, feat_width)
    block_rows = (live_mask * (flat_resid + attn_rows)).astype(jnp.bfloat16).reshape(group_size, length, feat_width)
    grad_res = live_mask * cot_rows.reshape(flat_count, feat_width).astype(jnp.float32)
    grad_low = grad_res.astype(jnp.bfloat16)
    grad_out = jnp.dot(mixed_rows.T, grad_low, preferred_element_type=jnp.float32)
    grad_mixed = jnp.dot(grad_low, out_weight.T, preferred_element_type=jnp.float32).astype(jnp.bfloat16)
    grad_mixed = grad_mixed.reshape(group_size, length, HEADS, head_dim)
    grad_probs = jnp.einsum('gihe,gjhe->ghij', grad_mixed.astype(jnp.float32), value_rows.astype(jnp.float32))
    inner_sum = lax.optimization_barrier(jnp.sum(prob_full * grad_probs, axis=-1, keepdims=True))
    grad_scores = (prob_full * (grad_probs - inner_sum) * score_scale).astype(jnp.bfloat16)
    grad_query = jnp.einsum('ghij,gjhe->gihe', grad_scores.astype(jnp.float32), key_rows.astype(jnp.float32)).astype(jnp.bfloat16)
    grad_key = jnp.einsum('ghij,gihe->gjhe', grad_scores.astype(jnp.float32), query_rows.astype(jnp.float32)).astype(jnp.bfloat16)
    grad_value = jnp.einsum('ghij,gihe->gjhe', probs_low.astype(jnp.float32), grad_mixed.astype(jnp.float32)).astype(jnp.bfloat16)
    grad_qkv = jnp.concatenate([grad_query.reshape(flat_count, feat_width), grad_key.reshape(flat_count, feat_width), grad_value.reshape(flat_count, feat_width)], axis=1)
    grad_in = jnp.dot(flat_normed.T, grad_qkv, preferred_element_type=jnp.float32)
    grad_normed = jnp.dot(grad_qkv, in_weight.T, preferred_element_type=jnp.float32)
    flat_inv = inv_rms.reshape(flat_count, 1)
    scaled = grad_normed * norm_gain
    grad_gain = lax.optimization_barrier(jnp.sum(grad_normed * flat_resid * flat_inv, axis=0))
    grad_resid = grad_res + flat_inv * scaled - flat_resid * (flat_inv * flat_inv * flat_inv) * lax.optimization_barrier(jnp.mean(scaled * flat_resid, axis=-1, keepdims=True))
    grad_pos = lax.optimization_barrier(jnp.sum(grad_resid.reshape(group_size, length, feat_width), axis=0))
    return (block_rows, (grad_in, grad_out, grad_gain, grad_pos))

def reference(item_table, neighbours, tile_weights, history, lengths, position, norm_gain, in_weight, out_weight, cotangent):
    table_tiles = item_table.reshape(NTILES, TILE, D)

    def one_tile(pair_args):
        tile_ids, tile_block = pair_args
        picked = table_tiles[tile_ids].astype(jnp.float32)
        return jnp.einsum('kab,kbd->ad', tile_block.astype(jnp.float32), picked)
    graph_term = lax.map(one_tile, (neighbours, tile_weights)).reshape(ITEMS, D)
    propagated = (0.5 * (item_table.astype(jnp.float32) + graph_term)).astype(jnp.bfloat16)

    def scan_step(totals, scan_args):
        hist_row, len_one, cot_one = scan_args
        fetched = propagated[hist_row]
        block_rows, grads = block_pass(fetched[None], len_one[None], cot_one[None], position, norm_gain, in_weight, out_weight)
        new_totals = tuple((total + grad for total, grad in zip(totals, grads)))
        return (new_totals, block_rows[0])
    start_totals = (jnp.zeros((D, 3 * D), jnp.float32), jnp.zeros((D, D), jnp.float32), jnp.zeros((D,), jnp.float32), jnp.zeros((L, D), jnp.float32))
    totals, block_out = lax.scan(scan_step, start_totals, (history, lengths, cotangent))
    return (block_out, totals[0], totals[1], totals[2], totals[3])
```

```python
import functools
import jax
import jax.numpy as jnp
from jax import lax
from jax.experimental import pallas as pl
from jax.experimental.pallas import tpu as pltpu
from jax.sharding import PartitionSpec as P

PART_TYPE = jnp.bfloat16
SPREAD_TYPE = jnp.bfloat16
HEADS = 8
BLK = 128
NT = (((1,), (1,)), ((), ()))
TN = (((0,), (0,)), ((), ()))


def dotf(a, b, dims=(((1,), (0,)), ((), ()))):
    return lax.dot_general(a, b, dims, preferred_element_type=jnp.float32)


def diag2(top, low):
    return jnp.concatenate(
        [
            jnp.concatenate([top, jnp.zeros_like(top)], axis=1),
            jnp.concatenate([jnp.zeros_like(low), low], axis=1),
        ],
        axis=0,
    )


def user_pass(
    n, live_len, x_ref, cot_ref, pos_ref, gain_ref, win_ref, wint_ref, wout_ref,
    blk_ref, gin_ref, gout_ref, ggain_ref, gpos_ref, gkt_ref, gvt_ref, mxt_ref, gqt_ref,
):
    feat = pos_ref.shape[1]
    hd = feat // HEADS
    scale = hd ** (-0.5)
    bf = jnp.bfloat16
    resid = x_ref[:n, :] + pos_ref[:n, :]
    inv = lax.rsqrt(jnp.mean(resid * resid, axis=1, keepdims=True) + 1e-05)
    gain = gain_ref[...]
    rnorm = resid * inv
    normed = (rnorm * gain).astype(bf)
    kv = dotf(normed, win_ref[:, feat:]).astype(bf)
    qkvt = dotf(wint_ref[...], normed, NT).astype(bf)
    live = lax.broadcasted_iota(jnp.int32, (n, feat), 0) < live_len
    gres = jnp.where(live, cot_ref[0, :n, :].astype(jnp.float32), 0.0)
    glow = gres.astype(bf)
    gmt = dotf(wout_ref[...], glow, NT).astype(bf)
    lane = lax.broadcasted_iota(jnp.int32, (BLK, 2 * BLK), 1)
    causal = lax.broadcasted_iota(jnp.int32, (BLK, 2 * BLK), 0) <= (lane & (BLK - 1))
    for pair in range(HEADS // 2):
        r0 = 2 * hd * pair
        quad = 128 * (r0 // 128)
        off = r0 - quad
        kq = kv[:, quad : quad + 128]
        vq = kv[:, feat + quad : feat + quad + 128]
        kt = qkvt[feat + r0 : feat + r0 + 2 * hd, :]
        vt = qkvt[2 * feat + r0 : 2 * feat + r0 + 2 * hd, :]
        for ib in range(n // BLK):
            i0 = ib * BLK
            nj = i0 + BLK
            qd = diag2(qkvt[r0 : r0 + hd, i0:nj], qkvt[r0 + hd : r0 + 2 * hd, i0:nj])
            md = diag2(gmt[r0 : r0 + hd, i0:nj], gmt[r0 + hd : r0 + 2 * hd, i0:nj])
            fill = jnp.zeros((2 * hd, 2 * BLK), bf)
            widen = lambda d: jnp.concatenate([d, fill] if off == 0 else [fill, d], axis=0)
            sc = dotf(kq[:nj], widen(qd)) * scale
            edge = jnp.where(causal, sc[i0:], -1e30)
            sc = edge if ib == 0 else jnp.concatenate([sc[:i0], edge], axis=0)
            top = jnp.max(sc, axis=0, keepdims=True)
            ex = jnp.exp(sc - top)
            prob = ex * (1.0 / jnp.sum(ex, axis=0, keepdims=True))
            plow = prob.astype(bf)
            mt = dotf(vt[:, :nj], plow)
            mxt_ref[r0 : r0 + hd, i0:nj] = mt[:hd, :BLK].astype(bf)
            mxt_ref[r0 + hd : r0 + 2 * hd, i0:nj] = mt[hd:, BLK:].astype(bf)
            gp = dotf(vq[:nj], widen(md))
            inner = jnp.sum(prob * gp, axis=0, keepdims=True)
            gs = (prob * (gp - inner) * scale).astype(bf)
            gq = dotf(kt[:, :nj], gs)
            gqt_ref[r0 : r0 + hd, i0:nj] = gq[:hd, :BLK].astype(bf)
            gqt_ref[r0 + hd : r0 + 2 * hd, i0:nj] = gq[hd:, BLK:].astype(bf)
            gk = dotf(qd, gs, NT)
            gv = dotf(md, plow, NT)
            if n > BLK and ib == 0:
                gkt_ref[r0 : r0 + 2 * hd, :] = gk
                gvt_ref[r0 : r0 + 2 * hd, :] = gv
            else:
                if ib > 0:
                    ones = [gkt_ref[r0 : r0 + 2 * hd, :], gvt_ref[r0 : r0 + 2 * hd, :]]
                    gk = jnp.concatenate([gk[:, :BLK] + ones[0], gk[:, BLK:]], axis=1)
                    gv = jnp.concatenate([gv[:, :BLK] + ones[1], gv[:, BLK:]], axis=1)
                gqt_ref[feat + r0 : feat + r0 + 2 * hd, :n] = gk.astype(bf)
                gqt_ref[2 * feat + r0 : 2 * feat + r0 + 2 * hd, :n] = gv.astype(bf)
    mxt = mxt_ref[:, :n]
    attn = dotf(mxt, wout_ref[...], TN)
    blk_ref[0, :n, :] = jnp.where(live, resid + attn, 0.0).astype(bf)
    if n < blk_ref.shape[1]:
        blk_ref[0, n:, :] = jnp.zeros((blk_ref.shape[1] - n, feat), bf)
    gout_ref[...] += dotf(mxt, glow)
    gqkvt = gqt_ref[:, :n]
    gin_ref[...] += dotf(gqkvt, normed)
    gn = dotf(win_ref[...], gqkvt).T
    scaled = gn * gain
    ggain_ref[...] += jnp.sum(gn * rnorm, axis=0, keepdims=True)
    corr = jnp.mean(scaled * resid, axis=1, keepdims=True) * (inv * inv * inv)
    gpos_ref[:n, :] += gres + inv * scaled - resid * corr


def attn_kernel(
    lens_ref, idx_ref, rows_ref, cot_ref, pos_ref, gain_ref, win_ref, wint_ref, wout_ref,
    blk_ref, pack_ref, rowf_ref, x_ref, gkt_ref, gvt_ref, mxt_ref, gqt_ref,
    gin_ref, gout_ref, ggain_ref, gpos_ref,
):
    u = pl.program_id(0)
    length = x_ref.shape[0]

    @pl.when(u == 0)
    def _():
        rowf_ref[...] = rows_ref[...].astype(jnp.float32)
        gin_ref[...] = jnp.zeros_like(gin_ref)
        gout_ref[...] = jnp.zeros_like(gout_ref)
        ggain_ref[...] = jnp.zeros_like(ggain_ref)
        gpos_ref[...] = jnp.zeros_like(gpos_ref)

    live_len = lens_ref[u]

    def run(n):
        def eight(g, carry):
            base = pl.multiple_of(g * 8, 8)
            for k in range(8):
                r = idx_ref[u * length + base + k]
                x_ref[pl.ds(base + k, 1), :] = rowf_ref[pl.ds(r, 1), :]
            return carry

        lax.fori_loop(0, n // 8, eight, 0)
        user_pass(
            n, live_len, x_ref, cot_ref, pos_ref, gain_ref, win_ref, wint_ref, wout_ref,
            blk_ref, gin_ref, gout_ref, ggain_ref, gpos_ref, gkt_ref, gvt_ref, mxt_ref, gqt_ref,
        )

    @pl.when(live_len <= BLK)
    def _():
        run(BLK)

    @pl.when(live_len > BLK)
    def _():
        run(length)

    @pl.when(u == pl.num_programs(0) - 1)
    def _():
        feat = gpos_ref.shape[1]
        gin = gin_ref[...].T
        at = 0
        for whole in (gin, gout_ref[...], gpos_ref[...]):
            for c in range(whole.shape[1] // 128):
                pack_ref[at : at + feat, :] = whole[:, 128 * c : 128 * c + 128].astype(pack_ref.dtype)
                at += feat
        tail = pack_ref.shape[0] - at
        pack_ref[at:, :] = jnp.zeros((tail, 128), pack_ref.dtype)
        row = lax.broadcasted_iota(jnp.int32, (16, 128), 0)
        gg = ggain_ref[...]
        both = jnp.where(row == 0, gg[:, :128], jnp.where(row == 1, gg[:, 128:], 0.0))
        pack_ref[at : at + 16, :] = both.astype(pack_ref.dtype)


def attention(rows, idx, lengths, cot, position, gain, win, wint, wout, pack_rows, pack_type):
    users, length, feat = cot.shape
    whole = lambda a: pl.BlockSpec(a.shape, lambda u, *_: (0,) * a.ndim, pipeline_mode=pl.Buffered(1))
    per_user = pl.BlockSpec((1, length, feat), lambda u, *_: (u, 0, 0))
    gain = gain.reshape(1, feat)
    f32, bf = jnp.float32, jnp.bfloat16
    return pl.pallas_call(
        attn_kernel,
        out_shape=(
            jax.ShapeDtypeStruct((users, length, feat), bf),
            jax.ShapeDtypeStruct((pack_rows, 128), pack_type),
        ),
        grid_spec=pltpu.PrefetchScalarGridSpec(
            num_scalar_prefetch=2,
            grid=(users,),
            in_specs=[whole(rows), per_user, whole(position), whole(gain), whole(win), whole(wint), whole(wout)],
            out_specs=[per_user, pl.BlockSpec((pack_rows, 128), lambda u, *_: (0, 0))],
            scratch_shapes=[
                pltpu.VMEM(rows.shape, f32),
                pltpu.VMEM((length, feat), f32),
                pltpu.VMEM((feat, BLK), f32),
                pltpu.VMEM((feat, BLK), f32),
                pltpu.VMEM((feat, length), bf),
                pltpu.VMEM((3 * feat, length), bf),
                pltpu.VMEM((3 * feat, feat), f32),
                pltpu.VMEM((feat, feat), f32),
                pltpu.VMEM((1, feat), f32),
                pltpu.VMEM((length, feat), f32),
            ],
        ),
        compiler_params=pltpu.CompilerParams(
            dimension_semantics=("arbitrary",), vmem_limit_bytes=48 * 2**20
        ),
    )(lengths, idx, rows, cot, position, gain, win, wint, wout)


def route_kernel(n_batch, n_item, hist_ref, sent_ref, place_ref):
    users, length = hist_ref.shape
    peers, per_peer = sent_ref.shape
    rows_own = 256
    f32, bf = jnp.float32, jnp.bfloat16
    peer_row = lax.broadcasted_iota(jnp.int32, (peers, length), 0)
    slot_row = lax.broadcasted_iota(jnp.int32, (per_peer, length), 0)
    before = (
        lax.broadcasted_iota(jnp.int32, (length, length), 0)
        < lax.broadcasted_iota(jnp.int32, (length, length), 1)
    ).astype(f32).astype(bf)
    counts = jnp.zeros((peers, 1), f32)
    sent = jnp.zeros((peers, per_peer), f32)
    for u in range(users):
        ids = hist_ref[u : u + 1, :]
        run = ids // rows_own
        owner = (run % n_batch) * n_item + run // n_batch
        inside = (ids % rows_own).astype(f32)
        mine = (peer_row == owner).astype(f32)
        ahead = dotf(mine.astype(bf), before) + counts
        rank = jnp.sum(mine * ahead, axis=0, keepdims=True)
        counts = counts + jnp.sum(mine, axis=1, keepdims=True)
        rank_int = rank.astype(jnp.int32)
        place_ref[u : u + 1, :] = owner * per_peer + rank_int
        slot = (slot_row == rank_int).astype(f32).astype(bf)
        sent = sent + dotf((mine * inside).astype(bf), slot, NT)
    sent_ref[...] = sent.astype(jnp.int32)


def route(history, n_batch, n_item):
    users, length = history.shape
    peers = n_batch * n_item
    per_peer = users * length // peers
    return pl.pallas_call(
        functools.partial(route_kernel, n_batch, n_item),
        out_shape=(
            jax.ShapeDtypeStruct((peers, per_peer), jnp.int32),
            jax.ShapeDtypeStruct((users, length), jnp.int32),
        ),
        name="route",
    )(history)


def graph_kernel(
    tile_ref, part_ref, left_ref, own_ref, right_ref, weights_ref, wanted_ref, found_ref, table, sems
):
    rows_item, feat = own_ref.shape
    tile = weights_ref.shape[-1]
    tiles_here = rows_item // tile
    copies = [
        pltpu.make_async_copy(src, table.at[pl.ds(i * rows_item, rows_item)], sems.at[i])
        for i, src in enumerate((left_ref, own_ref, right_ref))
    ]
    for c in copies:
        c.start()
    for c in copies:
        c.wait()
    groups, row_tiles, slots = weights_ref.shape[:3]

    def tile_of(g, n, k):
        place = tile_ref[(g * row_tiles + n) * slots + k]
        return table[pl.ds(pl.multiple_of(place * tile, tile), tile), :]

    halves = []
    for n in range(row_tiles):
        acc = jnp.zeros((tile, feat), jnp.float32)
        for g in range(groups):
            for k in range(0, slots, 2):
                lhs = jnp.concatenate([weights_ref[g, n, k], weights_ref[g, n, k + 1]], axis=1)
                rhs = jnp.concatenate([tile_of(g, n, k), tile_of(g, n, k + 1)], axis=0)
                acc = acc + dotf(lhs, rhs)
        start = pl.multiple_of(rows_item + (part_ref[0] * row_tiles + n) * tile, tile)
        own = table[pl.ds(start, tile), :].astype(jnp.float32)
        halves.append((0.5 * (own + acc)).astype(jnp.bfloat16))
    propagated = jnp.concatenate(halves, axis=0)
    columns = wanted_ref[...].astype(jnp.float32).T
    spot = lax.broadcasted_iota(jnp.int32, (128, row_tiles * tile), 1).astype(jnp.float32)
    for b in range(columns.shape[1]):
        pick = (columns[:, b : b + 1] == spot).astype(jnp.float32).astype(jnp.bfloat16)
        found_ref[128 * b : 128 * b + 128, :] = dotf(pick, propagated).astype(jnp.bfloat16)


def graph(tile_ids, part, left, own, right, weights, wanted):
    rows_item, feat = own.shape
    anywhere = pl.BlockSpec(memory_space=pl.ANY)
    whole = lambda a: pl.BlockSpec(a.shape, lambda i, *_: (0,) * a.ndim)
    count = wanted.shape[0] * wanted.shape[1]
    return pl.pallas_call(
        graph_kernel,
        out_shape=jax.ShapeDtypeStruct((count, feat), jnp.bfloat16),
        grid_spec=pltpu.PrefetchScalarGridSpec(
            num_scalar_prefetch=2,
            grid=(1,),
            in_specs=[anywhere, anywhere, anywhere, whole(weights), whole(wanted)],
            out_specs=pl.BlockSpec((count, feat), lambda i, *_: (0, 0)),
            scratch_shapes=[
                pltpu.VMEM((3 * rows_item, feat), jnp.bfloat16),
                pltpu.SemaphoreType.DMA((3,)),
            ],
        ),
        compiler_params=pltpu.CompilerParams(vmem_limit_bytes=40 * 2**20),
        name="graph",
    )(tile_ids, part, left, own, right, weights, wanted)


def sum_kernel(parts_ref, out_ref):
    total = jnp.sum(parts_ref[...].astype(jnp.float32), axis=0, keepdims=True)
    out_ref[...] = jnp.broadcast_to(total, out_ref.shape).astype(out_ref.dtype)


def sum_spread(parts, spread_type):
    return pl.pallas_call(
        sum_kernel,
        out_shape=jax.ShapeDtypeStruct(parts.shape, spread_type),
        compiler_params=pltpu.CompilerParams(vmem_limit_bytes=40 * 2**20),
        name="sum_spread",
    )(parts)


def exchange(cells, axes):
    return lax.all_to_all(cells, axes, split_axis=0, concat_axis=0, tiled=True)


def local(
    item_table, neighbours, tile_weights, history, lengths, position, norm_gain,
    in_weight, out_weight, cotangent,
):
    n_batch = lax.axis_size("batch")
    n_item = lax.axis_size("item")
    peers = n_batch * n_item
    everyone = ("batch", "item")
    rows_item, feat = item_table.shape
    tile = tile_weights.shape[2]
    tiles_here = rows_item // tile
    slots = tile_weights.shape[1]
    row_tiles = tiles_here // n_batch
    here = lax.axis_index("item")
    users_here, length = history.shape
    left = lax.ppermute(item_table, "item", [(i, (i + 1) % n_item) for i in range(n_item)])
    right = lax.ppermute(item_table, "item", [((i + 1) % n_item, i) for i in range(n_item)])
    weights = exchange(tile_weights, "batch").reshape(n_batch, row_tiles, slots, tile, tile)
    sent, place = route(history, n_batch, n_item)
    per_peer = sent.shape[1]
    rim = jnp.mod(neighbours - (here - 1) * tiles_here, n_item * tiles_here)
    rim = jnp.broadcast_to(
        rim.reshape(n_batch, 1, row_tiles * slots), (n_batch, n_item, row_tiles * slots)
    ).reshape(peers, row_tiles * slots)
    got = exchange(jnp.concatenate([sent, rim], axis=1), everyone)
    wanted = got[:, :per_peer].reshape(-1, 128)
    tile_ids = lax.dynamic_index_in_dim(
        got[:, per_peer:].reshape(n_batch, n_item, row_tiles * slots), here, 1, keepdims=False
    ).reshape(-1)
    part = lax.axis_index("batch").reshape(1)
    found = graph(tile_ids, part, left, item_table, right, weights, wanted)
    rows = exchange(found.reshape(peers, per_peer, feat), everyone).reshape(-1, feat)
    pack_rows = peers * 24
    block_out, packed = attention(
        rows, place.reshape(-1), lengths, cotangent, position, norm_gain, in_weight,
        in_weight.T, out_weight, pack_rows, PART_TYPE,
    )
    parts = exchange(packed.reshape(peers, pack_rows // peers, 128), everyone)
    full = exchange(sum_spread(parts, SPREAD_TYPE), everyone).reshape(pack_rows, 128)
    full = full.astype(jnp.float32)
    slab = lambda a, b: jnp.concatenate(
        [full[feat * i : feat * i + feat] for i in range(a, b)], axis=1
    )
    gain_row = 10 * feat
    return (
        block_out,
        slab(0, 6),
        slab(6, 8),
        full[gain_row : gain_row + 2].reshape(feat),
        slab(8, 10),
    )


def solution(mesh):
    in_specs = (
        P("item", None),
        P("item", "batch"),
        P("item", "batch", None, None),
        P(("batch", "item"), None),
        P(("batch", "item")),
        P(),
        P(),
        P(),
        P(),
        P(("batch", "item"), None, None),
    )
    out_specs = (P(("batch", "item"), None, None), P(), P(), P(), P())
    return jax.shard_map(local, mesh=mesh, in_specs=in_specs, out_specs=out_specs, check_vma=False)
```

```python
import functools
import math
import jax
import jax.numpy as jnp
from jax import lax
from jax.experimental import pallas as pl
from jax.experimental.pallas import tpu as pltpu
from jax.sharding import PartitionSpec as P

PART_TYPE = jnp.bfloat16
SPREAD_TYPE = jnp.bfloat16
HEADS = 8
BLK = 128
NT = (((1,), (1,)), ((), ()))
TN = (((0,), (0,)), ((), ()))


def dotf(a, b, dims=(((1,), (0,)), ((), ()))):
    return lax.dot_general(a, b, dims, preferred_element_type=jnp.float32)


def diag2(top, low):
    return jnp.concatenate(
        [
            jnp.concatenate([top, jnp.zeros_like(top)], axis=1),
            jnp.concatenate([jnp.zeros_like(low), low], axis=1),
        ],
        axis=0,
    )


def user_pass(
    n, live_len, x_ref, bring, cot_ref, pos_ref, gain_ref, win_ref, wint_ref, wout_ref,
    blk_ref, gin_ref, gout_ref, ggain_ref, gpos_ref, gkt_ref, gvt_ref, mxt_ref, gqt_ref, bias_ref,
):
    feat = pos_ref.shape[1]
    hd = feat // HEADS
    scale = hd ** (-0.5)
    bf = jnp.bfloat16
    resid = jnp.concatenate([x_ref[:n, 0, :], x_ref[:n, 1, :]], axis=1) + pos_ref[:n, :]
    inv = lax.rsqrt(jnp.mean(resid * resid, axis=1, keepdims=True) + 1e-05)
    gain = gain_ref[...]
    rnorm = resid * inv
    normed = (rnorm * gain).astype(bf)
    kv = dotf(normed, win_ref[:, feat:]).astype(bf)
    qkvt = dotf(wint_ref[...], normed, NT).astype(bf)
    live = lax.broadcasted_iota(jnp.int32, (n, feat), 0) < live_len
    gres = jnp.where(live, cot_ref[0, :n, :].astype(jnp.float32), 0.0)
    glow = gres.astype(bf)
    gmt = dotf(wout_ref[...], glow, NT).astype(bf)
    fill = jnp.zeros((2 * hd, 2 * BLK), bf)
    items = [(ib, pair) for ib in range(n // BLK) for pair in range(HEADS // 2)]

    def products(ib, pair):
        r0 = 2 * hd * pair
        quad = 128 * (r0 // 128)
        i0 = ib * BLK
        nj = i0 + BLK
        qd = diag2(qkvt[r0 : r0 + hd, i0:nj], qkvt[r0 + hd : r0 + 2 * hd, i0:nj])
        md = diag2(gmt[r0 : r0 + hd, i0:nj], gmt[r0 + hd : r0 + 2 * hd, i0:nj])
        widen = lambda d: jnp.concatenate([d, fill] if r0 == quad else [fill, d], axis=0)
        sc = dotf(kv[:nj, quad : quad + 128], widen(qd))
        gp = dotf(kv[:nj, feat + quad : feat + quad + 128], widen(md))
        return qd, md, sc, gp

    def soften(ib, pair, made):
        qd, md, sc, gp = made
        i0 = ib * BLK
        edge = sc[i0:] + bias_ref[...]
        sc = edge if ib == 0 else jnp.concatenate([sc[:i0], edge], axis=0)
        top = jnp.max(sc, axis=0, keepdims=True)
        ex = jnp.exp2((sc - top) * (scale * math.log2(math.e)))
        prob = ex * (1.0 / jnp.sum(ex, axis=0, keepdims=True))
        plow = prob.astype(bf)
        inner = jnp.sum(prob * gp, axis=0, keepdims=True)
        gs = (prob * (gp - inner)).astype(bf)
        return qd, md, plow, gs

    def collect(ib, pair, made):
        qd, md, plow, gs = made
        r0 = 2 * hd * pair
        i0 = ib * BLK
        nj = i0 + BLK
        kt = qkvt[feat + r0 : feat + r0 + 2 * hd, :nj]
        vt = qkvt[2 * feat + r0 : 2 * feat + r0 + 2 * hd, :nj]
        mt = dotf(vt, plow)
        gq = dotf(kt, gs)
        gk = dotf(qd, gs, NT) * scale
        gv = dotf(md, plow, NT)
        mxt_ref[r0 : r0 + hd, i0:nj] = mt[:hd, :BLK].astype(bf)
        mxt_ref[r0 + hd : r0 + 2 * hd, i0:nj] = mt[hd:, BLK:].astype(bf)
        gqt_ref[r0 : r0 + hd, i0:nj] = (gq[:hd, :BLK] * scale).astype(bf)
        gqt_ref[r0 + hd : r0 + 2 * hd, i0:nj] = (gq[hd:, BLK:] * scale).astype(bf)
        if n > BLK and ib == 0:
            gkt_ref[r0 : r0 + 2 * hd, :] = gk
            gvt_ref[r0 : r0 + 2 * hd, :] = gv
        else:
            if ib > 0:
                gk = jnp.concatenate([gk[:, :BLK] + gkt_ref[r0 : r0 + 2 * hd, :], gk[:, BLK:]], axis=1)
                gv = jnp.concatenate([gv[:, :BLK] + gvt_ref[r0 : r0 + 2 * hd, :], gv[:, BLK:]], axis=1)
            gqt_ref[feat + r0 : feat + r0 + 2 * hd, :n] = gk.astype(bf)
            gqt_ref[2 * feat + r0 : 2 * feat + r0 + 2 * hd, :n] = gv.astype(bf)

    made, soft = {}, {}
    for t in range(len(items) + 2):
        if t < len(items):
            bring(t, len(items))
            made[t] = products(*items[t])
        if t >= 2:
            collect(*items[t - 2], soft.pop(t - 2))
        s = t - 1
        if 0 <= s < len(items):
            soft[s] = soften(*items[s], made.pop(s))
    mxt = mxt_ref[:, :n]
    attn = dotf(mxt, wout_ref[...], TN)
    blk_ref[0, :n, :] = jnp.where(live, resid + attn, 0.0).astype(bf)
    if n < blk_ref.shape[1]:
        blk_ref[0, n:, :] = jnp.zeros((blk_ref.shape[1] - n, feat), bf)
    gout_ref[...] += dotf(mxt, glow)
    gqkvt = gqt_ref[:, :n]
    gin_ref[...] += dotf(gqkvt, normed)
    gn = dotf(win_ref[...], gqkvt).T
    scaled = gn * gain
    ggain_ref[...] += jnp.sum(gn * rnorm, axis=0, keepdims=True)
    corr = jnp.mean(scaled * resid, axis=1, keepdims=True) * (inv * inv * inv)
    gpos_ref[:n, :] += gres + inv * scaled - resid * corr


def attn_kernel(
    lens_ref, idx_ref, rows_ref, cot_ref, pos_ref, gain_ref, win_ref, wint_ref, wout_ref,
    out_ref, pack_ref, rowf_ref, x_ref, gkt_ref, gvt_ref, mxt_ref, gqt_ref,
    gin_ref, gout_ref, ggain_ref, gpos_ref, bias_ref, held_ref, sems,
):
    users, length, feat = cot_ref.shape

    def bring(user, first, count):
        for t in range(first, first + count, 16):
            some = [rowf_ref[idx_ref[user * length + t + k]] for k in range(16)]
            for k in range(16):
                x_ref[user % 2, t + k] = some[k]

    rowf_ref[:, 0, :] = rows_ref[:, :128].astype(jnp.float32)
    rowf_ref[:, 1, :] = rows_ref[:, 128:].astype(jnp.float32)
    bring(0, 0, length)
    gin_ref[...] = jnp.zeros_like(gin_ref)
    gout_ref[...] = jnp.zeros_like(gout_ref)
    ggain_ref[...] = jnp.zeros_like(ggain_ref)
    gpos_ref[...] = jnp.zeros_like(gpos_ref)
    lane = lax.broadcasted_iota(jnp.int32, (BLK, 2 * BLK), 1)
    row = lax.broadcasted_iota(jnp.int32, (BLK, 2 * BLK), 0)
    bias_ref[...] = jnp.where(row <= (lane & (BLK - 1)), 0.0, -1e30)

    def put(u):
        return pltpu.make_async_copy(held_ref.at[u % 2], out_ref.at[u], sems.at[u % 2])

    def step(u, carry):
        live_len = lens_ref[u]
        coming = jnp.minimum(u + 1, users - 1)

        @pl.when(u >= 2)
        def _():
            put(u - 2).wait()

        def run(n):
            user_pass(
                n, live_len, x_ref.at[u % 2],
                lambda t, of: bring(coming, t * length // of, length // of),
                cot_ref.at[pl.ds(u, 1)], pos_ref, gain_ref, win_ref, wint_ref, wout_ref,
                held_ref.at[pl.ds(u % 2, 1)], gin_ref, gout_ref, ggain_ref, gpos_ref,
                gkt_ref, gvt_ref, mxt_ref, gqt_ref, bias_ref,
            )

        @pl.when(live_len <= BLK)
        def _():
            run(BLK)

        @pl.when(live_len > BLK)
        def _():
            run(length)

        put(u).start()
        return carry

    lax.fori_loop(0, users, step, 0)
    gin = gin_ref[...].T
    at = 0
    for whole in (gin, gout_ref[...], gpos_ref[...]):
        for c in range(whole.shape[1] // 128):
            pack_ref[at : at + feat, :] = whole[:, 128 * c : 128 * c + 128].astype(pack_ref.dtype)
            at += feat
    tail = pack_ref.shape[0] - at
    pack_ref[at:, :] = jnp.zeros((tail, 128), pack_ref.dtype)
    top_row = lax.broadcasted_iota(jnp.int32, (16, 128), 0)
    gg = ggain_ref[...]
    both = jnp.where(top_row == 0, gg[:, :128], jnp.where(top_row == 1, gg[:, 128:], 0.0))
    pack_ref[at : at + 16, :] = both.astype(pack_ref.dtype)
    put(users - 2).wait()
    put(users - 1).wait()


def attention(rows, idx, lengths, cot, position, gain, win, wint, wout, pack_rows, pack_type):
    users, length, feat = cot.shape
    f32, bf = jnp.float32, jnp.bfloat16
    scalars = pl.BlockSpec(memory_space=pltpu.SMEM)
    near = pl.BlockSpec(memory_space=pltpu.VMEM)
    return pl.pallas_call(
        attn_kernel,
        out_shape=(
            jax.ShapeDtypeStruct((users, length, feat), bf),
            jax.ShapeDtypeStruct((pack_rows, 128), pack_type),
        ),
        in_specs=[scalars, scalars] + [near] * 7,
        out_specs=(pl.BlockSpec(memory_space=pl.ANY), near),
        scratch_shapes=[
            pltpu.VMEM((rows.shape[0], 2, 128), f32),
            pltpu.VMEM((2, length, 2, 128), f32),
            pltpu.VMEM((feat, BLK), f32),
            pltpu.VMEM((feat, BLK), f32),
            pltpu.VMEM((feat, length), bf),
            pltpu.VMEM((3 * feat, length), bf),
            pltpu.VMEM((3 * feat, feat), f32),
            pltpu.VMEM((feat, feat), f32),
            pltpu.VMEM((1, feat), f32),
            pltpu.VMEM((length, feat), f32),
            pltpu.VMEM((BLK, 2 * BLK), f32),
            pltpu.VMEM((2, length, feat), bf),
            pltpu.SemaphoreType.DMA((2,)),
        ],
        compiler_params=pltpu.CompilerParams(vmem_limit_bytes=40 * 2**20),
        name="attention",
    )(lengths, idx, rows, cot, position, gain.reshape(1, feat), win, wint, wout)


def route_kernel(n_batch, n_item, hist_ref, sent_ref, place_ref):
    users, length = hist_ref.shape
    peers, per_peer = sent_ref.shape
    rows_own = 256
    f32, bf = jnp.float32, jnp.bfloat16
    peer_row = lax.broadcasted_iota(jnp.int32, (peers, length), 0)
    slot_row = lax.broadcasted_iota(jnp.int32, (per_peer, length), 0)
    before = (
        lax.broadcasted_iota(jnp.int32, (length, length), 0)
        < lax.broadcasted_iota(jnp.int32, (length, length), 1)
    ).astype(f32).astype(bf)
    counts = jnp.zeros((peers, 1), f32)
    sent = jnp.zeros((peers, per_peer), f32)
    for u in range(users):
        ids = hist_ref[u : u + 1, :]
        run = ids // rows_own
        owner = (run % n_batch) * n_item + run // n_batch
        inside = (ids % rows_own).astype(f32)
        mine = (peer_row == owner).astype(f32)
        ahead = dotf(mine.astype(bf), before) + counts
        rank = jnp.sum(mine * ahead, axis=0, keepdims=True)
        counts = counts + jnp.sum(mine, axis=1, keepdims=True)
        rank_int = rank.astype(jnp.int32)
        place_ref[u : u + 1, :] = owner * per_peer + rank_int
        slot = (slot_row == rank_int).astype(f32).astype(bf)
        sent = sent + dotf((mine * inside).astype(bf), slot, NT)
    sent_ref[...] = sent.astype(jnp.int32)


def route(history, n_batch, n_item):
    users, length = history.shape
    peers = n_batch * n_item
    per_peer = users * length // peers
    return pl.pallas_call(
        functools.partial(route_kernel, n_batch, n_item),
        out_shape=(
            jax.ShapeDtypeStruct((peers, per_peer), jnp.int32),
            jax.ShapeDtypeStruct((users, length), jnp.int32),
        ),
        name="route",
    )(history)


def graph_kernel(
    tile_ref, part_ref, left_ref, own_ref, right_ref, held_ref, *refs
):
    arrived_refs = refs[: -5]
    wanted_ref, found_ref, table, weights_ref, sems = refs[-5:]
    rows_item, feat = own_ref.shape
    tile = weights_ref.shape[-1]
    groups, row_tiles, slots = weights_ref.shape[:3]
    part = part_ref[0]
    moves = [
        (src, table.at[pl.ds(i * rows_item, rows_item)])
        for i, src in enumerate((left_ref, own_ref, right_ref))
    ]
    moves.append((held_ref.at[pl.ds(part * row_tiles, row_tiles)], weights_ref.at[part]))
    for k, src in enumerate(arrived_refs):
        moves.append((src, weights_ref.at[lax.rem(part + groups - 1 - k, groups)]))
    copies = [
        pltpu.make_async_copy(src, dst, sems.at[i]) for i, (src, dst) in enumerate(moves)
    ]
    for c in copies:
        c.start()
    for c in copies:
        c.wait()

    def tile_of(g, n, k):
        place = tile_ref[(g * row_tiles + n) * slots + k]
        return table[pl.ds(pl.multiple_of(place * tile, tile), tile), :]

    halves = []
    for n in range(row_tiles):
        acc = jnp.zeros((tile, feat), jnp.float32)
        for g in range(groups):
            for k in range(0, slots, 2):
                lhs = jnp.concatenate([weights_ref[g, n, k], weights_ref[g, n, k + 1]], axis=1)
                rhs = jnp.concatenate([tile_of(g, n, k), tile_of(g, n, k + 1)], axis=0)
                acc = acc + dotf(lhs, rhs)
        start = pl.multiple_of(rows_item + (part * row_tiles + n) * tile, tile)
        own = table[pl.ds(start, tile), :].astype(jnp.float32)
        halves.append((0.5 * (own + acc)).astype(jnp.bfloat16))
    propagated = jnp.concatenate(halves, axis=0)
    columns = wanted_ref[...].astype(jnp.float32).T
    spot = lax.broadcasted_iota(jnp.int32, (128, row_tiles * tile), 1).astype(jnp.float32)
    for b in range(columns.shape[1]):
        pick = (columns[:, b : b + 1] == spot).astype(jnp.float32).astype(jnp.bfloat16)
        found_ref[128 * b : 128 * b + 128, :] = dotf(pick, propagated).astype(jnp.bfloat16)


def graph(tile_ids, part, left, own, right, held, arrived, wanted):
    rows_item, feat = own.shape
    count = wanted.shape[0] * wanted.shape[1]
    anywhere = pl.BlockSpec(memory_space=pl.ANY)
    scalars = pl.BlockSpec(memory_space=pltpu.SMEM)
    near = pl.BlockSpec(memory_space=pltpu.VMEM)
    block = arrived[0].shape
    return pl.pallas_call(
        graph_kernel,
        out_shape=jax.ShapeDtypeStruct((count, feat), jnp.bfloat16),
        in_specs=[scalars, scalars] + [anywhere] * (4 + len(arrived)) + [near],
        out_specs=near,
        scratch_shapes=[
            pltpu.VMEM((3 * rows_item, feat), jnp.bfloat16),
            pltpu.VMEM((1 + len(arrived),) + block, jnp.bfloat16),
            pltpu.SemaphoreType.DMA((4 + len(arrived),)),
        ],
        compiler_params=pltpu.CompilerParams(vmem_limit_bytes=40 * 2**20),
        name="graph",
    )(tile_ids, part, left, own, right, held, *arrived, wanted)


def sum_kernel(parts_ref, out_ref):
    total = jnp.sum(parts_ref[...].astype(jnp.float32), axis=0, keepdims=True)
    out_ref[...] = jnp.broadcast_to(total, out_ref.shape).astype(out_ref.dtype)


def sum_spread(parts, spread_type):
    return pl.pallas_call(
        sum_kernel,
        out_shape=jax.ShapeDtypeStruct(parts.shape, spread_type),
        compiler_params=pltpu.CompilerParams(vmem_limit_bytes=40 * 2**20),
        name="sum_spread",
    )(parts)


def exchange(cells, axes):
    return lax.all_to_all(cells, axes, split_axis=0, concat_axis=0, tiled=True)


def local(
    item_table, neighbours, tile_weights, history, lengths, position, norm_gain,
    in_weight, out_weight, cotangent,
):
    n_batch = lax.axis_size("batch")
    n_item = lax.axis_size("item")
    peers = n_batch * n_item
    everyone = ("batch", "item")
    rows_item, feat = item_table.shape
    tile = tile_weights.shape[2]
    tiles_here = rows_item // tile
    slots = tile_weights.shape[1]
    row_tiles = tiles_here // n_batch
    here = lax.axis_index("item")
    users_here, length = history.shape
    left = lax.ppermute(item_table, "item", [(i, (i + 1) % n_item) for i in range(n_item)])
    right = lax.ppermute(item_table, "item", [((i + 1) % n_item, i) for i in range(n_item)])
    mine = lax.axis_index("batch")
    arrived = []
    for k in range(1, n_batch):
        block = lax.dynamic_slice_in_dim(
            tile_weights, lax.rem(mine + k, n_batch) * row_tiles, row_tiles, 0
        )
        arrived.append(
            lax.ppermute(block, "batch", [(i, (i + k) % n_batch) for i in range(n_batch)])
        )
    sent, place = route(history, n_batch, n_item)
    per_peer = sent.shape[1]
    rim = jnp.mod(neighbours - (here - 1) * tiles_here, n_item * tiles_here)
    rim = jnp.broadcast_to(
        rim.reshape(n_batch, 1, row_tiles * slots), (n_batch, n_item, row_tiles * slots)
    ).reshape(peers, row_tiles * slots)
    got = exchange(jnp.concatenate([sent, rim], axis=1), everyone)
    wanted = got[:, :per_peer].reshape(-1, 128)
    tile_ids = lax.dynamic_index_in_dim(
        got[:, per_peer:].reshape(n_batch, n_item, row_tiles * slots), here, 1, keepdims=False
    ).reshape(-1)
    found = graph(tile_ids, mine.reshape(1), left, item_table, right, tile_weights, arrived, wanted)
    rows = exchange(found.reshape(peers, per_peer, feat), everyone).reshape(-1, feat)
    pack_rows = peers * 24
    block_out, packed = attention(
        rows, place.reshape(-1), lengths, cotangent, position, norm_gain, in_weight,
        in_weight.T, out_weight, pack_rows, PART_TYPE,
    )
    parts = exchange(packed.reshape(peers, pack_rows // peers, 128), everyone)
    full = exchange(sum_spread(parts, SPREAD_TYPE), everyone).reshape(pack_rows, 128)
    full = full.astype(jnp.float32)
    slab = lambda a, b: jnp.concatenate(
        [full[feat * i : feat * i + feat] for i in range(a, b)], axis=1
    )
    gain_row = 10 * feat
    return (
        block_out,
        slab(0, 6),
        slab(6, 8),
        full[gain_row : gain_row + 2].reshape(feat),
        slab(8, 10),
    )


def solution(mesh):
    in_specs = (
        P("item", None),
        P("item", "batch"),
        P("item", "batch", None, None),
        P(("batch", "item"), None),
        P(("batch", "item")),
        P(),
        P(),
        P(),
        P(),
        P(("batch", "item"), None, None),
    )
    out_specs = (P(("batch", "item"), None, None), P(), P(), P(), P())
    return jax.shard_map(local, mesh=mesh, in_specs=in_specs, out_specs=out_specs, check_vma=False)
```

```python
import functools
import math
import jax
import jax.numpy as jnp
from jax import lax
from jax.experimental import pallas as pl
from jax.experimental.pallas import tpu as pltpu
from jax.sharding import PartitionSpec as P

PART_TYPE = jnp.bfloat16
SPREAD_TYPE = jnp.bfloat16
HEADS = 8
BLK = 128
NT = (((1,), (1,)), ((), ()))
TN = (((0,), (0,)), ((), ()))


def dotf(a, b, dims=(((1,), (0,)), ((), ()))):
    return lax.dot_general(a, b, dims, preferred_element_type=jnp.float32)


def diag2(top, low):
    return jnp.concatenate(
        [
            jnp.concatenate([top, jnp.zeros_like(top)], axis=1),
            jnp.concatenate([jnp.zeros_like(low), low], axis=1),
        ],
        axis=0,
    )


def user_pass(
    n, live_len, x_ref, bring, cot_ref, pos_ref, gain_ref, win_ref, wint_ref, wout_ref,
    blk_ref, gin_ref, gout_ref, ggain_ref, gpos_ref, gkt_ref, gvt_ref, mxt_ref, gqt_ref, bias_ref,
):
    feat = pos_ref.shape[1]
    hd = feat // HEADS
    scale = hd ** (-0.5)
    bf = jnp.bfloat16
    resid = jnp.concatenate([x_ref[:n, 0, :], x_ref[:n, 1, :]], axis=1) + pos_ref[:n, :]
    inv = lax.rsqrt(jnp.mean(resid * resid, axis=1, keepdims=True) + 1e-05)
    gain = gain_ref[...]
    rnorm = resid * inv
    normed = (rnorm * gain).astype(bf)
    kv = dotf(normed, win_ref[:, feat:]).astype(bf)
    qkvt = dotf(wint_ref[...], normed, NT).astype(bf)
    live = lax.broadcasted_iota(jnp.int32, (n, feat), 0) < live_len
    gres = jnp.where(live, cot_ref[0, :n, :].astype(jnp.float32), 0.0)
    glow = gres.astype(bf)
    gmt = dotf(wout_ref[...], glow, NT).astype(bf)
    fill = jnp.zeros((2 * hd, 2 * BLK), bf)
    items = [(ib, pair) for ib in range(n // BLK) for pair in range(HEADS // 2)]

    def products(ib, pair):
        r0 = 2 * hd * pair
        quad = 128 * (r0 // 128)
        i0 = ib * BLK
        nj = i0 + BLK
        qd = diag2(qkvt[r0 : r0 + hd, i0:nj], qkvt[r0 + hd : r0 + 2 * hd, i0:nj])
        md = diag2(gmt[r0 : r0 + hd, i0:nj], gmt[r0 + hd : r0 + 2 * hd, i0:nj])
        widen = lambda d: jnp.concatenate([d, fill] if r0 == quad else [fill, d], axis=0)
        sc = dotf(kv[:nj, quad : quad + 128], widen(qd))
        gp = dotf(kv[:nj, feat + quad : feat + quad + 128], widen(md))
        return qd, md, sc, gp

    def soften(ib, pair, made):
        qd, md, sc, gp = made
        i0 = ib * BLK
        edge = sc[i0:] + bias_ref[...]
        sc = edge if ib == 0 else jnp.concatenate([sc[:i0], edge], axis=0)
        top = jnp.max(sc, axis=0, keepdims=True)
        ex = jnp.exp2((sc - top) * (scale * math.log2(math.e)))
        prob = ex * (1.0 / jnp.sum(ex, axis=0, keepdims=True))
        plow = prob.astype(bf)
        inner = jnp.sum(prob * gp, axis=0, keepdims=True)
        gs = (prob * (gp - inner)).astype(bf)
        return qd, md, plow, gs

    def collect(ib, pair, made):
        qd, md, plow, gs = made
        r0 = 2 * hd * pair
        i0 = ib * BLK
        nj = i0 + BLK
        kt = qkvt[feat + r0 : feat + r0 + 2 * hd, :nj]
        vt = qkvt[2 * feat + r0 : 2 * feat + r0 + 2 * hd, :nj]
        mt = dotf(vt, plow)
        gq = dotf(kt, gs)
        gk = dotf(qd, gs, NT) * scale
        gv = dotf(md, plow, NT)
        mxt_ref[r0 : r0 + hd, i0:nj] = mt[:hd, :BLK].astype(bf)
        mxt_ref[r0 + hd : r0 + 2 * hd, i0:nj] = mt[hd:, BLK:].astype(bf)
        gqt_ref[r0 : r0 + hd, i0:nj] = (gq[:hd, :BLK] * scale).astype(bf)
        gqt_ref[r0 + hd : r0 + 2 * hd, i0:nj] = (gq[hd:, BLK:] * scale).astype(bf)
        if n > BLK and ib == 0:
            gkt_ref[r0 : r0 + 2 * hd, :] = gk
            gvt_ref[r0 : r0 + 2 * hd, :] = gv
        else:
            if ib > 0:
                gk = jnp.concatenate([gk[:, :BLK] + gkt_ref[r0 : r0 + 2 * hd, :], gk[:, BLK:]], axis=1)
                gv = jnp.concatenate([gv[:, :BLK] + gvt_ref[r0 : r0 + 2 * hd, :], gv[:, BLK:]], axis=1)
            gqt_ref[feat + r0 : feat + r0 + 2 * hd, :n] = gk.astype(bf)
            gqt_ref[2 * feat + r0 : 2 * feat + r0 + 2 * hd, :n] = gv.astype(bf)

    made, soft = {}, {}
    for t in range(len(items) + 2):
        if t < len(items):
            bring(t, len(items))
            made[t] = products(*items[t])
        if t >= 2:
            collect(*items[t - 2], soft.pop(t - 2))
        s = t - 1
        if 0 <= s < len(items):
            soft[s] = soften(*items[s], made.pop(s))
    mxt = mxt_ref[:, :n]
    attn = dotf(mxt, wout_ref[...], TN)
    blk_ref[0, :n, :] = jnp.where(live, resid + attn, 0.0).astype(bf)
    if n < blk_ref.shape[1]:
        blk_ref[0, n:, :] = jnp.zeros((blk_ref.shape[1] - n, feat), bf)
    gout_ref[...] += dotf(mxt, glow)
    gqkvt = gqt_ref[:, :n]
    gin_ref[...] += dotf(gqkvt, normed)
    gn = dotf(win_ref[...], gqkvt).T
    scaled = gn * gain
    ggain_ref[...] += jnp.sum(gn * rnorm, axis=0, keepdims=True)
    corr = jnp.mean(scaled * resid, axis=1, keepdims=True) * (inv * inv * inv)
    gpos_ref[:n, :] += gres + inv * scaled - resid * corr


def attn_kernel(
    lens_ref, idx_ref, rows_ref, cot_ref, pos_ref, gain_ref, win_ref, wint_ref, wout_ref,
    out_ref, pack_ref, rowf_ref, x_ref, gkt_ref, gvt_ref, mxt_ref, gqt_ref,
    gin_ref, gout_ref, ggain_ref, gpos_ref, bias_ref, held_ref, sems,
):
    users, length, feat = cot_ref.shape

    def bring(user, first, count):
        for t in range(first, first + count, 16):
            some = [rowf_ref[idx_ref[user * length + t + k]] for k in range(16)]
            for k in range(16):
                x_ref[user % 2, t + k] = some[k]

    rowf_ref[:, 0, :] = rows_ref[:, :128].astype(jnp.float32)
    rowf_ref[:, 1, :] = rows_ref[:, 128:].astype(jnp.float32)
    bring(0, 0, length)
    gin_ref[...] = jnp.zeros_like(gin_ref)
    gout_ref[...] = jnp.zeros_like(gout_ref)
    ggain_ref[...] = jnp.zeros_like(ggain_ref)
    gpos_ref[...] = jnp.zeros_like(gpos_ref)
    lane = lax.broadcasted_iota(jnp.int32, (BLK, 2 * BLK), 1)
    row = lax.broadcasted_iota(jnp.int32, (BLK, 2 * BLK), 0)
    bias_ref[...] = jnp.where(row <= (lane & (BLK - 1)), 0.0, -1e30)

    def put(u):
        return pltpu.make_async_copy(held_ref.at[u % 2], out_ref.at[u], sems.at[u % 2])

    def step(u, carry):
        live_len = lens_ref[u]
        coming = jnp.minimum(u + 1, users - 1)

        @pl.when(u >= 2)
        def _():
            put(u - 2).wait()

        def run(n):
            user_pass(
                n, live_len, x_ref.at[u % 2],
                lambda t, of: bring(coming, t * length // of, length // of),
                cot_ref.at[pl.ds(u, 1)], pos_ref, gain_ref, win_ref, wint_ref, wout_ref,
                held_ref.at[pl.ds(u % 2, 1)], gin_ref, gout_ref, ggain_ref, gpos_ref,
                gkt_ref, gvt_ref, mxt_ref, gqt_ref, bias_ref,
            )

        @pl.when(live_len <= BLK)
        def _():
            run(BLK)

        @pl.when(live_len > BLK)
        def _():
            run(length)

        put(u).start()
        return carry

    lax.fori_loop(0, users, step, 0)
    gin = gin_ref[...].T
    at = 0
    for whole in (gin, gout_ref[...], gpos_ref[...]):
        for c in range(whole.shape[1] // 128):
            pack_ref[at : at + feat, :] = whole[:, 128 * c : 128 * c + 128].astype(pack_ref.dtype)
            at += feat
    tail = pack_ref.shape[0] - at
    pack_ref[at:, :] = jnp.zeros((tail, 128), pack_ref.dtype)
    top_row = lax.broadcasted_iota(jnp.int32, (16, 128), 0)
    gg = ggain_ref[...]
    both = jnp.where(top_row == 0, gg[:, :128], jnp.where(top_row == 1, gg[:, 128:], 0.0))
    pack_ref[at : at + 16, :] = both.astype(pack_ref.dtype)
    put(users - 2).wait()
    put(users - 1).wait()


def attention(rows, idx, lengths, cot, position, gain, win, wint, wout, pack_rows, pack_type):
    users, length, feat = cot.shape
    f32, bf = jnp.float32, jnp.bfloat16
    scalars = pl.BlockSpec(memory_space=pltpu.SMEM)
    near = pl.BlockSpec(memory_space=pltpu.VMEM)
    return pl.pallas_call(
        attn_kernel,
        out_shape=(
            jax.ShapeDtypeStruct((users, length, feat), bf),
            jax.ShapeDtypeStruct((pack_rows, 128), pack_type),
        ),
        in_specs=[scalars, scalars] + [near] * 7,
        out_specs=(pl.BlockSpec(memory_space=pl.ANY), near),
        scratch_shapes=[
            pltpu.VMEM((rows.shape[0], 2, 128), f32),
            pltpu.VMEM((2, length, 2, 128), f32),
            pltpu.VMEM((feat, BLK), f32),
            pltpu.VMEM((feat, BLK), f32),
            pltpu.VMEM((feat, length), bf),
            pltpu.VMEM((3 * feat, length), bf),
            pltpu.VMEM((3 * feat, feat), f32),
            pltpu.VMEM((feat, feat), f32),
            pltpu.VMEM((1, feat), f32),
            pltpu.VMEM((length, feat), f32),
            pltpu.VMEM((BLK, 2 * BLK), f32),
            pltpu.VMEM((2, length, feat), bf),
            pltpu.SemaphoreType.DMA((2,)),
        ],
        compiler_params=pltpu.CompilerParams(vmem_limit_bytes=40 * 2**20),
        name="attention",
    )(lengths, idx, rows, cot, position, gain.reshape(1, feat), win, wint, wout)


def route_kernel(n_batch, n_item, hist_ref, sent_ref, place_ref):
    users, length = hist_ref.shape
    peers, per_peer = sent_ref.shape
    rows_own = 256
    f32, bf = jnp.float32, jnp.bfloat16
    peer_row = lax.broadcasted_iota(jnp.int32, (peers, length), 0)
    slot_row = lax.broadcasted_iota(jnp.int32, (per_peer, length), 0)
    before = (
        lax.broadcasted_iota(jnp.int32, (length, length), 0)
        < lax.broadcasted_iota(jnp.int32, (length, length), 1)
    ).astype(f32).astype(bf)
    counts = jnp.zeros((peers, 1), f32)
    sent = jnp.zeros((peers, per_peer), f32)
    for u in range(users):
        ids = hist_ref[u : u + 1, :]
        run = ids // rows_own
        owner = (run % n_batch) * n_item + run // n_batch
        inside = (ids % rows_own).astype(f32)
        mine = (peer_row == owner).astype(f32)
        ahead = dotf(mine.astype(bf), before) + counts
        rank = jnp.sum(mine * ahead, axis=0, keepdims=True)
        counts = counts + jnp.sum(mine, axis=1, keepdims=True)
        rank_int = rank.astype(jnp.int32)
        place_ref[u : u + 1, :] = owner * per_peer + rank_int
        slot = (slot_row == rank_int).astype(f32).astype(bf)
        sent = sent + dotf((mine * inside).astype(bf), slot, NT)
    sent_ref[...] = sent.astype(jnp.int32)


def route(history, n_batch, n_item):
    users, length = history.shape
    peers = n_batch * n_item
    per_peer = users * length // peers
    return pl.pallas_call(
        functools.partial(route_kernel, n_batch, n_item),
        out_shape=(
            jax.ShapeDtypeStruct((peers, per_peer), jnp.int32),
            jax.ShapeDtypeStruct((users, length), jnp.int32),
        ),
        name="route",
    )(history)


def graph_kernel(
    tile_ref, part_ref, left_ref, own_ref, right_ref, held_ref, swapped_ref, *refs
):
    arrived_refs = refs[: -5]
    wanted_ref, found_ref, table, weights_ref, sems = refs[-5:]
    rows_item, feat = own_ref.shape
    tile = weights_ref.shape[-1]
    groups, row_tiles, slots = weights_ref.shape[:3]
    part = part_ref[0]
    moves = [
        (src, table.at[pl.ds(i * rows_item, rows_item)])
        for i, src in enumerate((left_ref, own_ref, right_ref))
    ]
    spot, side = part // 2, lax.rem(part, 2)
    chips = groups // 2
    moves.append((held_ref.at[spot, side], weights_ref.at[part]))
    moves.append((swapped_ref.at[spot], weights_ref.at[2 * spot + 1 - side]))
    for k, src in enumerate(arrived_refs):
        chip = lax.rem(spot + chips - 1 - k, chips)
        moves.append((src.at[0], weights_ref.at[2 * chip + side]))
        moves.append((src.at[1], weights_ref.at[2 * chip + 1 - side]))
    copies = [
        pltpu.make_async_copy(src, dst, sems.at[i]) for i, (src, dst) in enumerate(moves)
    ]
    for c in copies:
        c.start()
    for c in copies:
        c.wait()

    def tile_of(g, n, k):
        place = tile_ref[(g * row_tiles + n) * slots + k]
        return table[pl.ds(pl.multiple_of(place * tile, tile), tile), :]

    halves = []
    for n in range(row_tiles):
        acc = jnp.zeros((tile, feat), jnp.float32)
        for g in range(groups):
            for k in range(0, slots, 2):
                lhs = jnp.concatenate([weights_ref[g, n, k], weights_ref[g, n, k + 1]], axis=1)
                rhs = jnp.concatenate([tile_of(g, n, k), tile_of(g, n, k + 1)], axis=0)
                acc = acc + dotf(lhs, rhs)
        start = pl.multiple_of(rows_item + (part * row_tiles + n) * tile, tile)
        own = table[pl.ds(start, tile), :].astype(jnp.float32)
        halves.append((0.5 * (own + acc)).astype(jnp.bfloat16))
    propagated = jnp.concatenate(halves, axis=0)
    columns = wanted_ref[...].astype(jnp.float32).T
    spot = lax.broadcasted_iota(jnp.int32, (128, row_tiles * tile), 1).astype(jnp.float32)
    for b in range(columns.shape[1]):
        pick = (columns[:, b : b + 1] == spot).astype(jnp.float32).astype(jnp.bfloat16)
        found_ref[128 * b : 128 * b + 128, :] = dotf(pick, propagated).astype(jnp.bfloat16)


def graph(tile_ids, part, left, own, right, held, swapped, arrived, wanted):
    rows_item, feat = own.shape
    count = wanted.shape[0] * wanted.shape[1]
    anywhere = pl.BlockSpec(memory_space=pl.ANY)
    scalars = pl.BlockSpec(memory_space=pltpu.SMEM)
    near = pl.BlockSpec(memory_space=pltpu.VMEM)
    groups = 2 * held.shape[0]
    return pl.pallas_call(
        graph_kernel,
        out_shape=jax.ShapeDtypeStruct((count, feat), jnp.bfloat16),
        in_specs=[scalars, scalars] + [anywhere] * (5 + len(arrived)) + [near],
        out_specs=near,
        scratch_shapes=[
            pltpu.VMEM((3 * rows_item, feat), jnp.bfloat16),
            pltpu.VMEM((groups,) + held.shape[2:], jnp.bfloat16),
            pltpu.SemaphoreType.DMA((3 + groups,)),
        ],
        compiler_params=pltpu.CompilerParams(vmem_limit_bytes=40 * 2**20),
        name="graph",
    )(tile_ids, part, left, own, right, held, swapped, *arrived, wanted)


def sum_kernel(parts_ref, out_ref):
    total = jnp.sum(parts_ref[...].astype(jnp.float32), axis=0, keepdims=True)
    out_ref[...] = jnp.broadcast_to(total, out_ref.shape).astype(out_ref.dtype)


def sum_spread(parts, spread_type):
    return pl.pallas_call(
        sum_kernel,
        out_shape=jax.ShapeDtypeStruct(parts.shape, spread_type),
        compiler_params=pltpu.CompilerParams(vmem_limit_bytes=40 * 2**20),
        name="sum_spread",
    )(parts)


def exchange(cells, axes):
    return lax.all_to_all(cells, axes, split_axis=0, concat_axis=0, tiled=True)


def local(
    item_table, neighbours, tile_weights, history, lengths, position, norm_gain,
    in_weight, out_weight, cotangent,
):
    n_batch = lax.axis_size("batch")
    n_item = lax.axis_size("item")
    peers = n_batch * n_item
    everyone = ("batch", "item")
    rows_item, feat = item_table.shape
    tile = tile_weights.shape[2]
    tiles_here = rows_item // tile
    slots = tile_weights.shape[1]
    row_tiles = tiles_here // n_batch
    here = lax.axis_index("item")
    users_here, length = history.shape
    left = lax.ppermute(item_table, "item", [(i, (i + 1) % n_item) for i in range(n_item)])
    right = lax.ppermute(item_table, "item", [((i + 1) % n_item, i) for i in range(n_item)])
    mine = lax.axis_index("batch")
    spot, side = mine // 2, lax.rem(mine, 2)
    chips = n_batch // 2
    by_owner = tile_weights.reshape(chips, 2, row_tiles, slots, tile, tile)
    swapped = lax.ppermute(
        lax.dynamic_index_in_dim(by_owner, 1 - side, 1, keepdims=False),
        "batch",
        [(i, i ^ 1) for i in range(n_batch)],
    )
    arrived = []
    for k in range(1, chips):
        chip = lax.rem(spot + k, chips)
        own_part = lax.dynamic_slice(
            by_owner, (chip, side, 0, 0, 0, 0), (1, 1, row_tiles, slots, tile, tile)
        )[0]
        pair = jnp.concatenate([own_part, lax.dynamic_slice_in_dim(swapped, chip, 1, 0)], axis=0)
        arrived.append(
            lax.ppermute(pair, "batch", [(i, (i + 2 * k) % n_batch) for i in range(n_batch)])
        )
    sent, place = route(history, n_batch, n_item)
    per_peer = sent.shape[1]
    rim = jnp.mod(neighbours - (here - 1) * tiles_here, n_item * tiles_here)
    rim = jnp.broadcast_to(
        rim.reshape(n_batch, 1, row_tiles * slots), (n_batch, n_item, row_tiles * slots)
    ).reshape(peers, row_tiles * slots)
    got = exchange(jnp.concatenate([sent, rim], axis=1), everyone)
    wanted = got[:, :per_peer].reshape(-1, 128)
    tile_ids = lax.dynamic_index_in_dim(
        got[:, per_peer:].reshape(n_batch, n_item, row_tiles * slots), here, 1, keepdims=False
    ).reshape(-1)
    found = graph(tile_ids, mine.reshape(1), left, item_table, right, by_owner, swapped, arrived, wanted)
    rows = exchange(found.reshape(peers, per_peer, feat), everyone).reshape(-1, feat)
    pack_rows = peers * 24
    block_out, packed = attention(
        rows, place.reshape(-1), lengths, cotangent, position, norm_gain, in_weight,
        in_weight.T, out_weight, pack_rows, PART_TYPE,
    )
    parts = exchange(packed.reshape(peers, pack_rows // peers, 128), everyone)
    full = exchange(sum_spread(parts, SPREAD_TYPE), everyone).reshape(pack_rows, 128)
    full = full.astype(jnp.float32)
    slab = lambda a, b: jnp.concatenate(
        [full[feat * i : feat * i + feat] for i in range(a, b)], axis=1
    )
    gain_row = 10 * feat
    return (
        block_out,
        slab(0, 6),
        slab(6, 8),
        full[gain_row : gain_row + 2].reshape(feat),
        slab(8, 10),
    )


def solution(mesh):
    in_specs = (
        P("item", None),
        P("item", "batch"),
        P("item", "batch", None, None),
        P(("batch", "item"), None),
        P(("batch", "item")),
        P(),
        P(),
        P(),
        P(),
        P(("batch", "item"), None, None),
    )
    out_specs = (P(("batch", "item"), None, None), P(), P(), P(), P())
    return jax.shard_map(local, mesh=mesh, in_specs=in_specs, out_specs=out_specs, check_vma=False)
```

```python
import functools
import math
import jax
import jax.numpy as jnp
from jax import lax
from jax.experimental import pallas as pl
from jax.experimental.pallas import tpu as pltpu
from jax.sharding import PartitionSpec as P

PART_TYPE = jnp.bfloat16
SPREAD_TYPE = jnp.bfloat16
HEADS = 8
BLK = 128
NT = (((1,), (1,)), ((), ()))
TN = (((0,), (0,)), ((), ()))


def dotf(a, b, dims=(((1,), (0,)), ((), ()))):
    return lax.dot_general(a, b, dims, preferred_element_type=jnp.float32)


def diag2(top, low):
    return jnp.concatenate(
        [
            jnp.concatenate([top, jnp.zeros_like(top)], axis=1),
            jnp.concatenate([jnp.zeros_like(low), low], axis=1),
        ],
        axis=0,
    )


def pair_pass(
    extents, lives, x_ref, bring, cot_ref, pos_ref, gain_ref, win_ref, wint_ref, wout_ref,
    blk_ref, gin_ref, gout_ref, ggain_ref, gpos_ref, gkt_ref, gvt_ref, mxt_ref, gqt_ref, bias_ref,
):
    feat = pos_ref.shape[1]
    hd = feat // HEADS
    scale = hd ** (-0.5)
    bf = jnp.bfloat16
    gain = gain_ref[...]
    state = {}

    def head(w):
        n = extents[w]
        resid = jnp.concatenate([x_ref[w, :n, 0, :], x_ref[w, :n, 1, :]], axis=1) + pos_ref[:n, :]
        inv = lax.rsqrt(jnp.mean(resid * resid, axis=1, keepdims=True) + 1e-05)
        rnorm = resid * inv
        normed = (rnorm * gain).astype(bf)
        kv = dotf(normed, win_ref[:, feat:]).astype(bf)
        qkvt = dotf(wint_ref[...], normed, NT).astype(bf)
        live = lax.broadcasted_iota(jnp.int32, (n, feat), 0) < lives[w]
        gres = jnp.where(live, cot_ref[w, :n, :].astype(jnp.float32), 0.0)
        glow = gres.astype(bf)
        gmt = dotf(wout_ref[...], glow, NT).astype(bf)
        state[w] = (resid, inv, rnorm, normed, kv, qkvt, live, gres, glow, gmt)

    def products(w, ib, pair):
        kv, qkvt, gmt = state[w][4], state[w][5], state[w][9]
        r0 = 2 * hd * pair
        quad = 128 * (r0 // 128)
        i0 = ib * BLK
        nj = i0 + BLK
        fill = jnp.zeros((2 * hd, 2 * BLK), bf)
        qd = diag2(qkvt[r0 : r0 + hd, i0:nj], qkvt[r0 + hd : r0 + 2 * hd, i0:nj])
        md = diag2(gmt[r0 : r0 + hd, i0:nj], gmt[r0 + hd : r0 + 2 * hd, i0:nj])
        widen = lambda d: jnp.concatenate([d, fill] if r0 == quad else [fill, d], axis=0)
        sc = dotf(kv[:nj, quad : quad + 128], widen(qd))
        gp = dotf(kv[:nj, feat + quad : feat + quad + 128], widen(md))
        return qd, md, sc, gp

    def soften(w, ib, pair, made):
        qd, md, sc, gp = made
        i0 = ib * BLK
        edge = sc[i0:] + bias_ref[...]
        sc = edge if ib == 0 else jnp.concatenate([sc[:i0], edge], axis=0)
        top = jnp.max(sc, axis=0, keepdims=True)
        ex = jnp.exp2((sc - top) * (scale * math.log2(math.e)))
        prob = ex * (1.0 / jnp.sum(ex, axis=0, keepdims=True))
        plow = prob.astype(bf)
        inner = jnp.sum(prob * gp, axis=0, keepdims=True)
        gs = (prob * (gp - inner)).astype(bf)
        return qd, md, plow, gs

    def collect(w, ib, pair, made):
        n = extents[w]
        qkvt = state[w][5]
        qd, md, plow, gs = made
        r0 = 2 * hd * pair
        i0 = ib * BLK
        nj = i0 + BLK
        kt = qkvt[feat + r0 : feat + r0 + 2 * hd, :nj]
        vt = qkvt[2 * feat + r0 : 2 * feat + r0 + 2 * hd, :nj]
        mt = dotf(vt, plow)
        gq = dotf(kt, gs)
        gk = dotf(qd, gs, NT) * scale
        gv = dotf(md, plow, NT)
        mxt_ref[w, r0 : r0 + hd, i0:nj] = mt[:hd, :BLK].astype(bf)
        mxt_ref[w, r0 + hd : r0 + 2 * hd, i0:nj] = mt[hd:, BLK:].astype(bf)
        gqt_ref[w, r0 : r0 + hd, i0:nj] = (gq[:hd, :BLK] * scale).astype(bf)
        gqt_ref[w, r0 + hd : r0 + 2 * hd, i0:nj] = (gq[hd:, BLK:] * scale).astype(bf)
        if n > BLK and ib == 0:
            gkt_ref[w, r0 : r0 + 2 * hd, :] = gk
            gvt_ref[w, r0 : r0 + 2 * hd, :] = gv
        else:
            if ib > 0:
                gk = jnp.concatenate([gk[:, :BLK] + gkt_ref[w, r0 : r0 + 2 * hd, :], gk[:, BLK:]], axis=1)
                gv = jnp.concatenate([gv[:, :BLK] + gvt_ref[w, r0 : r0 + 2 * hd, :], gv[:, BLK:]], axis=1)
            gqt_ref[w, feat + r0 : feat + r0 + 2 * hd, :n] = gk.astype(bf)
            gqt_ref[w, 2 * feat + r0 : 2 * feat + r0 + 2 * hd, :n] = gv.astype(bf)

    def tail(w):
        n = extents[w]
        resid, inv, rnorm, normed, kv, qkvt, live, gres, glow, gmt = state[w]
        mxt = mxt_ref[w, :, :n]
        attn = dotf(mxt, wout_ref[...], TN)
        blk_ref[w, :n, :] = jnp.where(live, resid + attn, 0.0).astype(bf)
        if n < blk_ref.shape[1]:
            blk_ref[w, n:, :] = jnp.zeros((blk_ref.shape[1] - n, feat), bf)
        gout_ref[...] += dotf(mxt, glow)
        gqkvt = gqt_ref[w, :, :n]
        gin_ref[...] += dotf(gqkvt, normed)
        gn = dotf(win_ref[...], gqkvt).T
        scaled = gn * gain
        ggain_ref[...] += jnp.sum(gn * rnorm, axis=0, keepdims=True)
        corr = jnp.mean(scaled * resid, axis=1, keepdims=True) * (inv * inv * inv)
        gpos_ref[:n, :] += gres + inv * scaled - resid * corr

    items = [
        (w, ib, pair)
        for w in range(len(extents))
        for ib in range(extents[w] // BLK)
        for pair in range(HEADS // 2)
    ]
    first = len([i for i in items if i[0] == 0])
    made, soft = {}, {}
    head(0)
    for t in range(len(items) + 2):
        if t < len(items):
            bring(t, len(items))
            if t == 3:
                head(1)
            made[t] = products(*items[t])
        if t >= 2:
            collect(*items[t - 2], soft.pop(t - 2))
        if t - 2 == first - 1 + 2:
            tail(0)
        s = t - 1
        if 0 <= s < len(items):
            soft[s] = soften(*items[s], made.pop(s))
    tail(1)


def attn_kernel(
    lens_ref, idx_ref, rows_ref, cot_ref, pos_ref, gain_ref, win_ref, wint_ref, wout_ref,
    out_ref, pack_ref, rowf_ref, x_ref, gkt_ref, gvt_ref, mxt_ref, gqt_ref,
    gin_ref, gout_ref, ggain_ref, gpos_ref, bias_ref, held_ref, sems,
):
    users, length, feat = cot_ref.shape

    def bring(pair, first, count):
        for t in range(first, first + count, 16):
            some = [rowf_ref[idx_ref[pair * 2 * length + t + k]] for k in range(16)]
            for k in range(16):
                x_ref[pair % 2, (t + k) // length, (t + k) % length] = some[k]

    rowf_ref[:, 0, :] = rows_ref[:, :128].astype(jnp.float32)
    rowf_ref[:, 1, :] = rows_ref[:, 128:].astype(jnp.float32)
    bring(0, 0, 2 * length)
    gin_ref[...] = jnp.zeros_like(gin_ref)
    gout_ref[...] = jnp.zeros_like(gout_ref)
    ggain_ref[...] = jnp.zeros_like(ggain_ref)
    gpos_ref[...] = jnp.zeros_like(gpos_ref)
    lane = lax.broadcasted_iota(jnp.int32, (BLK, 2 * BLK), 1)
    row = lax.broadcasted_iota(jnp.int32, (BLK, 2 * BLK), 0)
    bias_ref[...] = jnp.where(row <= (lane & (BLK - 1)), 0.0, -1e30)

    def put(p):
        return pltpu.make_async_copy(
            held_ref.at[p % 2], out_ref.at[pl.ds(2 * p, 2)], sems.at[p % 2]
        )

    pairs = users // 2

    def step(p, carry):
        lives = (lens_ref[2 * p], lens_ref[2 * p + 1])
        coming = jnp.minimum(p + 1, pairs - 1)

        @pl.when(p >= 2)
        def _():
            put(p - 2).wait()

        def run(extents):
            def fetch(t, of):
                part = [16 * (2 * length // 16 * i // of) for i in (t, t + 1)]
                bring(coming, part[0], part[1] - part[0])

            pair_pass(
                extents, lives, x_ref.at[p % 2], fetch,
                cot_ref.at[pl.ds(2 * p, 2)], pos_ref, gain_ref, win_ref, wint_ref, wout_ref,
                held_ref.at[p % 2], gin_ref, gout_ref, ggain_ref, gpos_ref,
                gkt_ref, gvt_ref, mxt_ref, gqt_ref, bias_ref,
            )

        for a in (BLK, length):
            for b in (BLK, length):
                fits = (lives[0] <= BLK) == (a == BLK)
                fits &= (lives[1] <= BLK) == (b == BLK)
                pl.when(fits)(functools.partial(run, (a, b)))

        put(p).start()
        return carry

    lax.fori_loop(0, pairs, step, 0)
    gin = gin_ref[...].T
    at = 0
    for whole in (gin, gout_ref[...], gpos_ref[...]):
        for c in range(whole.shape[1] // 128):
            pack_ref[at : at + feat, :] = whole[:, 128 * c : 128 * c + 128].astype(pack_ref.dtype)
            at += feat
    tail = pack_ref.shape[0] - at
    pack_ref[at:, :] = jnp.zeros((tail, 128), pack_ref.dtype)
    top_row = lax.broadcasted_iota(jnp.int32, (16, 128), 0)
    gg = ggain_ref[...]
    both = jnp.where(top_row == 0, gg[:, :128], jnp.where(top_row == 1, gg[:, 128:], 0.0))
    pack_ref[at : at + 16, :] = both.astype(pack_ref.dtype)
    put(pairs - 2).wait()
    put(pairs - 1).wait()


def attention(rows, idx, lengths, cot, position, gain, win, wint, wout, pack_rows, pack_type):
    users, length, feat = cot.shape
    f32, bf = jnp.float32, jnp.bfloat16
    scalars = pl.BlockSpec(memory_space=pltpu.SMEM)
    near = pl.BlockSpec(memory_space=pltpu.VMEM)
    return pl.pallas_call(
        attn_kernel,
        out_shape=(
            jax.ShapeDtypeStruct((users, length, feat), bf),
            jax.ShapeDtypeStruct((pack_rows, 128), pack_type),
        ),
        in_specs=[scalars, scalars] + [near] * 7,
        out_specs=(pl.BlockSpec(memory_space=pl.ANY), near),
        scratch_shapes=[
            pltpu.VMEM((rows.shape[0], 2, 128), f32),
            pltpu.VMEM((2, 2, length, 2, 128), f32),
            pltpu.VMEM((2, feat, BLK), f32),
            pltpu.VMEM((2, feat, BLK), f32),
            pltpu.VMEM((2, feat, length), bf),
            pltpu.VMEM((2, 3 * feat, length), bf),
            pltpu.VMEM((3 * feat, feat), f32),
            pltpu.VMEM((feat, feat), f32),
            pltpu.VMEM((1, feat), f32),
            pltpu.VMEM((length, feat), f32),
            pltpu.VMEM((BLK, 2 * BLK), f32),
            pltpu.VMEM((2, 2, length, feat), bf),
            pltpu.SemaphoreType.DMA((2,)),
        ],
        compiler_params=pltpu.CompilerParams(vmem_limit_bytes=40 * 2**20),
        name="attention",
    )(lengths, idx, rows, cot, position, gain.reshape(1, feat), win, wint, wout)


def route_kernel(n_batch, n_item, hist_ref, sent_ref, place_ref):
    users, length = hist_ref.shape
    peers, per_peer = sent_ref.shape
    rows_own = 256
    f32, bf = jnp.float32, jnp.bfloat16
    peer_row = lax.broadcasted_iota(jnp.int32, (peers, length), 0)
    slot_row = lax.broadcasted_iota(jnp.int32, (per_peer, length), 0)
    before = (
        lax.broadcasted_iota(jnp.int32, (length, length), 0)
        < lax.broadcasted_iota(jnp.int32, (length, length), 1)
    ).astype(f32).astype(bf)
    counts = jnp.zeros((peers, 1), f32)
    sent = jnp.zeros((peers, per_peer), f32)
    for u in range(users):
        ids = hist_ref[u : u + 1, :]
        run = ids // rows_own
        owner = (run % n_batch) * n_item + run // n_batch
        inside = (ids % rows_own).astype(f32)
        mine = (peer_row == owner).astype(f32)
        ahead = dotf(mine.astype(bf), before) + counts
        rank = jnp.sum(mine * ahead, axis=0, keepdims=True)
        counts = counts + jnp.sum(mine, axis=1, keepdims=True)
        rank_int = rank.astype(jnp.int32)
        place_ref[u : u + 1, :] = owner * per_peer + rank_int
        slot = (slot_row == rank_int).astype(f32).astype(bf)
        sent = sent + dotf((mine * inside).astype(bf), slot, NT)
    sent_ref[...] = sent.astype(jnp.int32)


def route(history, n_batch, n_item):
    users, length = history.shape
    peers = n_batch * n_item
    per_peer = users * length // peers
    return pl.pallas_call(
        functools.partial(route_kernel, n_batch, n_item),
        out_shape=(
            jax.ShapeDtypeStruct((peers, per_peer), jnp.int32),
            jax.ShapeDtypeStruct((users, length), jnp.int32),
        ),
        name="route",
    )(history)


def graph_kernel(
    tile_ref, part_ref, left_ref, own_ref, right_ref, held_ref, swapped_ref, *refs
):
    arrived_refs = refs[: -5]
    wanted_ref, found_ref, table, weights_ref, sems = refs[-5:]
    rows_item, feat = own_ref.shape
    tile = weights_ref.shape[-1]
    groups, row_tiles, slots = weights_ref.shape[:3]
    part = part_ref[0]
    moves = [
        (src, table.at[pl.ds(i * rows_item, rows_item)])
        for i, src in enumerate((left_ref, own_ref, right_ref))
    ]
    spot, side = part // 2, lax.rem(part, 2)
    chips = groups // 2
    moves.append((held_ref.at[spot, side], weights_ref.at[part]))
    moves.append((swapped_ref.at[spot], weights_ref.at[2 * spot + 1 - side]))
    for k, src in enumerate(arrived_refs):
        chip = lax.rem(spot + chips - 1 - k, chips)
        moves.append((src.at[0], weights_ref.at[2 * chip + side]))
        moves.append((src.at[1], weights_ref.at[2 * chip + 1 - side]))
    copies = [
        pltpu.make_async_copy(src, dst, sems.at[i]) for i, (src, dst) in enumerate(moves)
    ]
    for c in copies:
        c.start()
    for c in copies:
        c.wait()

    def tile_of(g, n, k):
        place = tile_ref[(g * row_tiles + n) * slots + k]
        return table[pl.ds(pl.multiple_of(place * tile, tile), tile), :]

    halves = []
    for n in range(row_tiles):
        acc = jnp.zeros((tile, feat), jnp.float32)
        for g in range(groups):
            for k in range(0, slots, 2):
                lhs = jnp.concatenate([weights_ref[g, n, k], weights_ref[g, n, k + 1]], axis=1)
                rhs = jnp.concatenate([tile_of(g, n, k), tile_of(g, n, k + 1)], axis=0)
                acc = acc + dotf(lhs, rhs)
        start = pl.multiple_of(rows_item + (part * row_tiles + n) * tile, tile)
        own = table[pl.ds(start, tile), :].astype(jnp.float32)
        halves.append((0.5 * (own + acc)).astype(jnp.bfloat16))
    propagated = jnp.concatenate(halves, axis=0)
    columns = wanted_ref[...].astype(jnp.float32).T
    spot = lax.broadcasted_iota(jnp.int32, (128, row_tiles * tile), 1).astype(jnp.float32)
    for b in range(columns.shape[1]):
        pick = (columns[:, b : b + 1] == spot).astype(jnp.float32).astype(jnp.bfloat16)
        found_ref[128 * b : 128 * b + 128, :] = dotf(pick, propagated).astype(jnp.bfloat16)


def graph(tile_ids, part, left, own, right, held, swapped, arrived, wanted):
    rows_item, feat = own.shape
    count = wanted.shape[0] * wanted.shape[1]
    anywhere = pl.BlockSpec(memory_space=pl.ANY)
    scalars = pl.BlockSpec(memory_space=pltpu.SMEM)
    near = pl.BlockSpec(memory_space=pltpu.VMEM)
    groups = 2 * held.shape[0]
    return pl.pallas_call(
        graph_kernel,
        out_shape=jax.ShapeDtypeStruct((count, feat), jnp.bfloat16),
        in_specs=[scalars, scalars] + [anywhere] * (5 + len(arrived)) + [near],
        out_specs=near,
        scratch_shapes=[
            pltpu.VMEM((3 * rows_item, feat), jnp.bfloat16),
            pltpu.VMEM((groups,) + held.shape[2:], jnp.bfloat16),
            pltpu.SemaphoreType.DMA((3 + groups,)),
        ],
        compiler_params=pltpu.CompilerParams(vmem_limit_bytes=40 * 2**20),
        name="graph",
    )(tile_ids, part, left, own, right, held, swapped, *arrived, wanted)


def sum_kernel(parts_ref, out_ref):
    total = jnp.sum(parts_ref[...].astype(jnp.float32), axis=0, keepdims=True)
    out_ref[...] = jnp.broadcast_to(total, out_ref.shape).astype(out_ref.dtype)


def sum_spread(parts, spread_type):
    return pl.pallas_call(
        sum_kernel,
        out_shape=jax.ShapeDtypeStruct(parts.shape, spread_type),
        compiler_params=pltpu.CompilerParams(vmem_limit_bytes=40 * 2**20),
        name="sum_spread",
    )(parts)


def exchange(cells, axes):
    return lax.all_to_all(cells, axes, split_axis=0, concat_axis=0, tiled=True)


def local(
    item_table, neighbours, tile_weights, history, lengths, position, norm_gain,
    in_weight, out_weight, cotangent,
):
    n_batch = lax.axis_size("batch")
    n_item = lax.axis_size("item")
    peers = n_batch * n_item
    everyone = ("batch", "item")
    rows_item, feat = item_table.shape
    tile = tile_weights.shape[2]
    tiles_here = rows_item // tile
    slots = tile_weights.shape[1]
    row_tiles = tiles_here // n_batch
    here = lax.axis_index("item")
    users_here, length = history.shape
    left = lax.ppermute(item_table, "item", [(i, (i + 1) % n_item) for i in range(n_item)])
    right = lax.ppermute(item_table, "item", [((i + 1) % n_item, i) for i in range(n_item)])
    mine = lax.axis_index("batch")
    spot, side = mine // 2, lax.rem(mine, 2)
    chips = n_batch // 2
    by_owner = tile_weights.reshape(chips, 2, row_tiles, slots, tile, tile)
    swapped = lax.ppermute(
        lax.dynamic_index_in_dim(by_owner, 1 - side, 1, keepdims=False),
        "batch",
        [(i, i ^ 1) for i in range(n_batch)],
    )
    arrived = []
    for k in range(1, chips):
        chip = lax.rem(spot + k, chips)
        own_part = lax.dynamic_slice(
            by_owner, (chip, side, 0, 0, 0, 0), (1, 1, row_tiles, slots, tile, tile)
        )[0]
        pair = jnp.concatenate([own_part, lax.dynamic_slice_in_dim(swapped, chip, 1, 0)], axis=0)
        arrived.append(
            lax.ppermute(pair, "batch", [(i, (i + 2 * k) % n_batch) for i in range(n_batch)])
        )
    sent, place = route(history, n_batch, n_item)
    per_peer = sent.shape[1]
    rim = jnp.mod(neighbours - (here - 1) * tiles_here, n_item * tiles_here)
    rim = jnp.broadcast_to(
        rim.reshape(n_batch, 1, row_tiles * slots), (n_batch, n_item, row_tiles * slots)
    ).reshape(peers, row_tiles * slots)
    got = exchange(jnp.concatenate([sent, rim], axis=1), everyone)
    wanted = got[:, :per_peer].reshape(-1, 128)
    tile_ids = lax.dynamic_index_in_dim(
        got[:, per_peer:].reshape(n_batch, n_item, row_tiles * slots), here, 1, keepdims=False
    ).reshape(-1)
    found = graph(tile_ids, mine.reshape(1), left, item_table, right, by_owner, swapped, arrived, wanted)
    rows = exchange(found.reshape(peers, per_peer, feat), everyone).reshape(-1, feat)
    pack_rows = peers * 24
    block_out, packed = attention(
        rows, place.reshape(-1), lengths, cotangent, position, norm_gain, in_weight,
        in_weight.T, out_weight, pack_rows, PART_TYPE,
    )
    parts = exchange(packed.reshape(peers, pack_rows // peers, 128), everyone)
    full = exchange(sum_spread(parts, SPREAD_TYPE), everyone).reshape(pack_rows, 128)
    full = full.astype(jnp.float32)
    slab = lambda a, b: jnp.concatenate(
        [full[feat * i : feat * i + feat] for i in range(a, b)], axis=1
    )
    gain_row = 10 * feat
    return (
        block_out,
        slab(0, 6),
        slab(6, 8),
        full[gain_row : gain_row + 2].reshape(feat),
        slab(8, 10),
    )


def solution(mesh):
    in_specs = (
        P("item", None),
        P("item", "batch"),
        P("item", "batch", None, None),
        P(("batch", "item"), None),
        P(("batch", "item")),
        P(),
        P(),
        P(),
        P(),
        P(("batch", "item"), None, None),
    )
    out_specs = (P(("batch", "item"), None, None), P(), P(), P(), P())
    return jax.shard_map(local, mesh=mesh, in_specs=in_specs, out_specs=out_specs, check_vma=False)
```

```python
import functools
import math
import jax
import jax.numpy as jnp
from jax import lax
from jax.experimental import pallas as pl
from jax.experimental.pallas import tpu as pltpu
from jax.sharding import PartitionSpec as P

PART_TYPE = jnp.bfloat16
SPREAD_TYPE = jnp.bfloat16
HEADS = 8
BLK = 128
NT = (((1,), (1,)), ((), ()))
TN = (((0,), (0,)), ((), ()))


def dotf(a, b, dims=(((1,), (0,)), ((), ()))):
    return lax.dot_general(a, b, dims, preferred_element_type=jnp.float32)


def diag2(top, low):
    return jnp.concatenate(
        [
            jnp.concatenate([top, jnp.zeros_like(top)], axis=1),
            jnp.concatenate([jnp.zeros_like(low), low], axis=1),
        ],
        axis=0,
    )


def pair_pass(
    extents, lives, x_ref, bring, cot_ref, pos_ref, gain_ref, win_ref, wint_ref, wout_ref,
    blk_ref, gin_ref, gout_ref, ggain_ref, gpos_ref, gkt_ref, gvt_ref, mxt_ref, gqt_ref, bias_ref,
):
    feat = pos_ref.shape[1]
    hd = feat // HEADS
    scale = hd ** (-0.5)
    bf = jnp.bfloat16
    gain = gain_ref[...]
    state = {}

    def head(w):
        n = extents[w]
        resid = jnp.concatenate([x_ref[w, :n, 0, :], x_ref[w, :n, 1, :]], axis=1) + pos_ref[:n, :]
        inv = lax.rsqrt(jnp.mean(resid * resid, axis=1, keepdims=True) + 1e-05)
        rnorm = resid * inv
        normed = (rnorm * gain).astype(bf)
        kv = dotf(normed, win_ref[:, feat:]).astype(bf)
        qkvt = dotf(wint_ref[...], normed, NT).astype(bf)
        live = lax.broadcasted_iota(jnp.int32, (n, feat), 0) < lives[w]
        gres = jnp.where(live, cot_ref[w, :n, :].astype(jnp.float32), 0.0)
        glow = gres.astype(bf)
        gmt = dotf(wout_ref[...], glow, NT).astype(bf)
        state[w] = (resid, inv, rnorm, normed, kv, qkvt, live, gres, glow, gmt)

    def products(w, ib, pair):
        kv, qkvt, gmt = state[w][4], state[w][5], state[w][9]
        r0 = 2 * hd * pair
        quad = 128 * (r0 // 128)
        i0 = ib * BLK
        nj = i0 + BLK
        fill = jnp.zeros((2 * hd, 2 * BLK), bf)
        qd = diag2(qkvt[r0 : r0 + hd, i0:nj], qkvt[r0 + hd : r0 + 2 * hd, i0:nj])
        md = diag2(gmt[r0 : r0 + hd, i0:nj], gmt[r0 + hd : r0 + 2 * hd, i0:nj])
        widen = lambda d: jnp.concatenate([d, fill] if r0 == quad else [fill, d], axis=0)
        sc = dotf(kv[:nj, quad : quad + 128], widen(qd))
        gp = dotf(kv[:nj, feat + quad : feat + quad + 128], widen(md))
        return qd, md, sc, gp

    def soften(w, ib, pair, made):
        qd, md, sc, gp = made
        i0 = ib * BLK
        edge = sc[i0:] + bias_ref[...]
        sc = edge if ib == 0 else jnp.concatenate([sc[:i0], edge], axis=0)
        top = jnp.max(sc, axis=0, keepdims=True)
        ex = jnp.exp2((sc - top) * (scale * math.log2(math.e)))
        prob = ex * (1.0 / jnp.sum(ex, axis=0, keepdims=True))
        plow = prob.astype(bf)
        inner = jnp.sum(prob * gp, axis=0, keepdims=True)
        gs = (prob * (gp - inner)).astype(bf)
        return qd, md, plow, gs

    def collect(w, ib, pair, made):
        n = extents[w]
        qkvt = state[w][5]
        qd, md, plow, gs = made
        r0 = 2 * hd * pair
        i0 = ib * BLK
        nj = i0 + BLK
        kt = qkvt[feat + r0 : feat + r0 + 2 * hd, :nj]
        vt = qkvt[2 * feat + r0 : 2 * feat + r0 + 2 * hd, :nj]
        mt = dotf(vt, plow)
        gq = dotf(kt, gs)
        gk = dotf(qd, gs, NT) * scale
        gv = dotf(md, plow, NT)
        mxt_ref[w, r0 : r0 + hd, i0:nj] = mt[:hd, :BLK].astype(bf)
        mxt_ref[w, r0 + hd : r0 + 2 * hd, i0:nj] = mt[hd:, BLK:].astype(bf)
        gqt_ref[w, r0 : r0 + hd, i0:nj] = (gq[:hd, :BLK] * scale).astype(bf)
        gqt_ref[w, r0 + hd : r0 + 2 * hd, i0:nj] = (gq[hd:, BLK:] * scale).astype(bf)
        if n > BLK and ib == 0:
            gkt_ref[w, r0 : r0 + 2 * hd, :] = gk
            gvt_ref[w, r0 : r0 + 2 * hd, :] = gv
        else:
            if ib > 0:
                gk = jnp.concatenate([gk[:, :BLK] + gkt_ref[w, r0 : r0 + 2 * hd, :], gk[:, BLK:]], axis=1)
                gv = jnp.concatenate([gv[:, :BLK] + gvt_ref[w, r0 : r0 + 2 * hd, :], gv[:, BLK:]], axis=1)
            gqt_ref[w, feat + r0 : feat + r0 + 2 * hd, :n] = gk.astype(bf)
            gqt_ref[w, 2 * feat + r0 : 2 * feat + r0 + 2 * hd, :n] = gv.astype(bf)

    def tail(w):
        n = extents[w]
        resid, inv, rnorm, normed, kv, qkvt, live, gres, glow, gmt = state[w]
        mxt = mxt_ref[w, :, :n]
        attn = dotf(mxt, wout_ref[...], TN)
        blk_ref[w, :n, :] = jnp.where(live, resid + attn, 0.0).astype(bf)
        if n < blk_ref.shape[1]:
            blk_ref[w, n:, :] = jnp.zeros((blk_ref.shape[1] - n, feat), bf)
        gout_ref[...] += dotf(mxt, glow)
        gqkvt = gqt_ref[w, :, :n]
        gin_ref[...] += dotf(gqkvt, normed)
        gn = dotf(win_ref[...], gqkvt).T
        scaled = gn * gain
        ggain_ref[...] += jnp.sum(gn * rnorm, axis=0, keepdims=True)
        corr = jnp.mean(scaled * resid, axis=1, keepdims=True) * (inv * inv * inv)
        gpos_ref[:n, :] += gres + inv * scaled - resid * corr

    items = [
        (w, ib, pair)
        for w in range(len(extents))
        for ib in range(extents[w] // BLK)
        for pair in range(HEADS // 2)
    ]
    first = len([i for i in items if i[0] == 0])
    made, soft = {}, {}
    head(0)
    for t in range(len(items) + 2):
        if 0 <= t - 1 < len(items):
            soft[t - 1] = soften(*items[t - 1], made.pop(t - 1))
        if t < len(items):
            bring(t, len(items))
            if t == 3:
                head(1)
            made[t] = products(*items[t])
        if t >= 2:
            collect(*items[t - 2], soft.pop(t - 2))
        if t - 2 == first - 1 + 2:
            tail(0)
    tail(1)


def attn_kernel(
    lens_ref, idx_ref, rows_ref, cot_ref, pos_ref, gain_ref, win_ref, wint_ref, wout_ref,
    out_ref, pack_ref, rowf_ref, x_ref, gkt_ref, gvt_ref, mxt_ref, gqt_ref,
    gin_ref, gout_ref, ggain_ref, gpos_ref, bias_ref, held_ref, sems,
):
    users, length, feat = cot_ref.shape

    def bring(pair, first, count):
        for t in range(first, first + count, 16):
            some = [rowf_ref[idx_ref[pair * 2 * length + t + k]] for k in range(16)]
            for k in range(16):
                x_ref[pair % 2, (t + k) // length, (t + k) % length] = some[k]

    rowf_ref[:, 0, :] = rows_ref[:, :128].astype(jnp.float32)
    rowf_ref[:, 1, :] = rows_ref[:, 128:].astype(jnp.float32)
    bring(0, 0, 2 * length)
    gin_ref[...] = jnp.zeros_like(gin_ref)
    gout_ref[...] = jnp.zeros_like(gout_ref)
    ggain_ref[...] = jnp.zeros_like(ggain_ref)
    gpos_ref[...] = jnp.zeros_like(gpos_ref)
    lane = lax.broadcasted_iota(jnp.int32, (BLK, 2 * BLK), 1)
    row = lax.broadcasted_iota(jnp.int32, (BLK, 2 * BLK), 0)
    bias_ref[...] = jnp.where(row <= (lane & (BLK - 1)), 0.0, -1e30)

    def put(p):
        return pltpu.make_async_copy(
            held_ref.at[p % 2], out_ref.at[pl.ds(2 * p, 2)], sems.at[p % 2]
        )

    pairs = users // 2

    def step(p, carry):
        lives = (lens_ref[2 * p], lens_ref[2 * p + 1])
        coming = jnp.minimum(p + 1, pairs - 1)

        @pl.when(p >= 2)
        def _():
            put(p - 2).wait()

        def run(extents):
            def fetch(t, of):
                part = [16 * (2 * length // 16 * i // of) for i in (t, t + 1)]
                bring(coming, part[0], part[1] - part[0])

            pair_pass(
                extents, lives, x_ref.at[p % 2], fetch,
                cot_ref.at[pl.ds(2 * p, 2)], pos_ref, gain_ref, win_ref, wint_ref, wout_ref,
                held_ref.at[p % 2], gin_ref, gout_ref, ggain_ref, gpos_ref,
                gkt_ref, gvt_ref, mxt_ref, gqt_ref, bias_ref,
            )

        for a in (BLK, length):
            for b in (BLK, length):
                fits = (lives[0] <= BLK) == (a == BLK)
                fits &= (lives[1] <= BLK) == (b == BLK)
                pl.when(fits)(functools.partial(run, (a, b)))

        put(p).start()
        return carry

    lax.fori_loop(0, pairs, step, 0)
    gin = gin_ref[...].T
    at = 0
    for whole in (gin, gout_ref[...], gpos_ref[...]):
        for c in range(whole.shape[1] // 128):
            pack_ref[at : at + feat, :] = whole[:, 128 * c : 128 * c + 128].astype(pack_ref.dtype)
            at += feat
    tail = pack_ref.shape[0] - at
    pack_ref[at:, :] = jnp.zeros((tail, 128), pack_ref.dtype)
    top_row = lax.broadcasted_iota(jnp.int32, (16, 128), 0)
    gg = ggain_ref[...]
    both = jnp.where(top_row == 0, gg[:, :128], jnp.where(top_row == 1, gg[:, 128:], 0.0))
    pack_ref[at : at + 16, :] = both.astype(pack_ref.dtype)
    put(pairs - 2).wait()
    put(pairs - 1).wait()


def attention(rows, idx, lengths, cot, position, gain, win, wint, wout, pack_rows, pack_type):
    users, length, feat = cot.shape
    f32, bf = jnp.float32, jnp.bfloat16
    scalars = pl.BlockSpec(memory_space=pltpu.SMEM)
    near = pl.BlockSpec(memory_space=pltpu.VMEM)
    return pl.pallas_call(
        attn_kernel,
        out_shape=(
            jax.ShapeDtypeStruct((users, length, feat), bf),
            jax.ShapeDtypeStruct((pack_rows, 128), pack_type),
        ),
        in_specs=[scalars, scalars] + [near] * 7,
        out_specs=(pl.BlockSpec(memory_space=pl.ANY), near),
        scratch_shapes=[
            pltpu.VMEM((rows.shape[0], 2, 128), f32),
            pltpu.VMEM((2, 2, length, 2, 128), f32),
            pltpu.VMEM((2, feat, BLK), f32),
            pltpu.VMEM((2, feat, BLK), f32),
            pltpu.VMEM((2, feat, length), bf),
            pltpu.VMEM((2, 3 * feat, length), bf),
            pltpu.VMEM((3 * feat, feat), f32),
            pltpu.VMEM((feat, feat), f32),
            pltpu.VMEM((1, feat), f32),
            pltpu.VMEM((length, feat), f32),
            pltpu.VMEM((BLK, 2 * BLK), f32),
            pltpu.VMEM((2, 2, length, feat), bf),
            pltpu.SemaphoreType.DMA((2,)),
        ],
        compiler_params=pltpu.CompilerParams(vmem_limit_bytes=40 * 2**20),
        name="attention",
    )(lengths, idx, rows, cot, position, gain.reshape(1, feat), win, wint, wout)


def route_kernel(n_batch, n_item, hist_ref, sent_ref, place_ref):
    users, length = hist_ref.shape
    peers, per_peer = sent_ref.shape
    rows_own = 256
    f32, bf = jnp.float32, jnp.bfloat16
    peer_row = lax.broadcasted_iota(jnp.int32, (peers, length), 0)
    slot_row = lax.broadcasted_iota(jnp.int32, (per_peer, length), 0)
    before = (
        lax.broadcasted_iota(jnp.int32, (length, length), 0)
        < lax.broadcasted_iota(jnp.int32, (length, length), 1)
    ).astype(f32).astype(bf)
    counts = jnp.zeros((peers, 1), f32)
    sent = jnp.zeros((peers, per_peer), f32)
    for u in range(users):
        ids = hist_ref[u : u + 1, :]
        run = ids // rows_own
        owner = (run % n_batch) * n_item + run // n_batch
        inside = (ids % rows_own).astype(f32)
        mine = (peer_row == owner).astype(f32)
        ahead = dotf(mine.astype(bf), before) + counts
        rank = jnp.sum(mine * ahead, axis=0, keepdims=True)
        counts = counts + jnp.sum(mine, axis=1, keepdims=True)
        rank_int = rank.astype(jnp.int32)
        place_ref[u : u + 1, :] = owner * per_peer + rank_int
        slot = (slot_row == rank_int).astype(f32).astype(bf)
        sent = sent + dotf((mine * inside).astype(bf), slot, NT)
    sent_ref[...] = sent.astype(jnp.int32)


def route(history, n_batch, n_item):
    users, length = history.shape
    peers = n_batch * n_item
    per_peer = users * length // peers
    return pl.pallas_call(
        functools.partial(route_kernel, n_batch, n_item),
        out_shape=(
            jax.ShapeDtypeStruct((peers, per_peer), jnp.int32),
            jax.ShapeDtypeStruct((users, length), jnp.int32),
        ),
        name="route",
    )(history)


def graph_kernel(
    tile_ref, part_ref, left_ref, own_ref, right_ref, held_ref, swapped_ref, *refs
):
    arrived_refs = refs[: -5]
    wanted_ref, found_ref, table, weights_ref, sems = refs[-5:]
    rows_item, feat = own_ref.shape
    tile = weights_ref.shape[-1]
    groups, row_tiles, slots = weights_ref.shape[:3]
    part = part_ref[0]
    moves = [
        (src, table.at[pl.ds(i * rows_item, rows_item)])
        for i, src in enumerate((left_ref, own_ref, right_ref))
    ]
    spot, side = part // 2, lax.rem(part, 2)
    chips = groups // 2
    moves.append((held_ref.at[spot, side], weights_ref.at[part]))
    moves.append((swapped_ref.at[spot], weights_ref.at[2 * spot + 1 - side]))
    for k, src in enumerate(arrived_refs):
        chip = lax.rem(spot + chips - 1 - k, chips)
        moves.append((src.at[0], weights_ref.at[2 * chip + side]))
        moves.append((src.at[1], weights_ref.at[2 * chip + 1 - side]))
    copies = [
        pltpu.make_async_copy(src, dst, sems.at[i]) for i, (src, dst) in enumerate(moves)
    ]
    for c in copies:
        c.start()
    for c in copies:
        c.wait()

    def tile_of(g, n, k):
        place = tile_ref[(g * row_tiles + n) * slots + k]
        return table[pl.ds(pl.multiple_of(place * tile, tile), tile), :]

    halves = []
    for n in range(row_tiles):
        acc = jnp.zeros((tile, feat), jnp.float32)
        for g in range(groups):
            for k in range(0, slots, 2):
                lhs = jnp.concatenate([weights_ref[g, n, k], weights_ref[g, n, k + 1]], axis=1)
                rhs = jnp.concatenate([tile_of(g, n, k), tile_of(g, n, k + 1)], axis=0)
                acc = acc + dotf(lhs, rhs)
        start = pl.multiple_of(rows_item + (part * row_tiles + n) * tile, tile)
        own = table[pl.ds(start, tile), :].astype(jnp.float32)
        halves.append((0.5 * (own + acc)).astype(jnp.bfloat16))
    propagated = jnp.concatenate(halves, axis=0)
    columns = wanted_ref[...].astype(jnp.float32).T
    spot = lax.broadcasted_iota(jnp.int32, (128, row_tiles * tile), 1).astype(jnp.float32)
    for b in range(columns.shape[1]):
        pick = (columns[:, b : b + 1] == spot).astype(jnp.float32).astype(jnp.bfloat16)
        found_ref[128 * b : 128 * b + 128, :] = dotf(pick, propagated).astype(jnp.bfloat16)


def graph(tile_ids, part, left, own, right, held, swapped, arrived, wanted):
    rows_item, feat = own.shape
    count = wanted.shape[0] * wanted.shape[1]
    anywhere = pl.BlockSpec(memory_space=pl.ANY)
    scalars = pl.BlockSpec(memory_space=pltpu.SMEM)
    near = pl.BlockSpec(memory_space=pltpu.VMEM)
    groups = 2 * held.shape[0]
    return pl.pallas_call(
        graph_kernel,
        out_shape=jax.ShapeDtypeStruct((count, feat), jnp.bfloat16),
        in_specs=[scalars, scalars] + [anywhere] * (5 + len(arrived)) + [near],
        out_specs=near,
        scratch_shapes=[
            pltpu.VMEM((3 * rows_item, feat), jnp.bfloat16),
            pltpu.VMEM((groups,) + held.shape[2:], jnp.bfloat16),
            pltpu.SemaphoreType.DMA((3 + groups,)),
        ],
        compiler_params=pltpu.CompilerParams(vmem_limit_bytes=40 * 2**20),
        name="graph",
    )(tile_ids, part, left, own, right, held, swapped, *arrived, wanted)


def sum_kernel(parts_ref, out_ref):
    total = jnp.sum(parts_ref[...].astype(jnp.float32), axis=0, keepdims=True)
    out_ref[...] = jnp.broadcast_to(total, out_ref.shape).astype(out_ref.dtype)


def sum_spread(parts, spread_type):
    return pl.pallas_call(
        sum_kernel,
        out_shape=jax.ShapeDtypeStruct(parts.shape, spread_type),
        compiler_params=pltpu.CompilerParams(vmem_limit_bytes=40 * 2**20),
        name="sum_spread",
    )(parts)


def exchange(cells, axes):
    return lax.all_to_all(cells, axes, split_axis=0, concat_axis=0, tiled=True)


def local(
    item_table, neighbours, tile_weights, history, lengths, position, norm_gain,
    in_weight, out_weight, cotangent,
):
    n_batch = lax.axis_size("batch")
    n_item = lax.axis_size("item")
    peers = n_batch * n_item
    everyone = ("batch", "item")
    rows_item, feat = item_table.shape
    tile = tile_weights.shape[2]
    tiles_here = rows_item // tile
    slots = tile_weights.shape[1]
    row_tiles = tiles_here // n_batch
    here = lax.axis_index("item")
    users_here, length = history.shape
    left = lax.ppermute(item_table, "item", [(i, (i + 1) % n_item) for i in range(n_item)])
    right = lax.ppermute(item_table, "item", [((i + 1) % n_item, i) for i in range(n_item)])
    mine = lax.axis_index("batch")
    spot, side = mine // 2, lax.rem(mine, 2)
    chips = n_batch // 2
    by_owner = tile_weights.reshape(chips, 2, row_tiles, slots, tile, tile)
    swapped = lax.ppermute(
        lax.dynamic_index_in_dim(by_owner, 1 - side, 1, keepdims=False),
        "batch",
        [(i, i ^ 1) for i in range(n_batch)],
    )
    arrived = []
    for k in range(1, chips):
        chip = lax.rem(spot + k, chips)
        own_part = lax.dynamic_slice(
            by_owner, (chip, side, 0, 0, 0, 0), (1, 1, row_tiles, slots, tile, tile)
        )[0]
        pair = jnp.concatenate([own_part, lax.dynamic_slice_in_dim(swapped, chip, 1, 0)], axis=0)
        arrived.append(
            lax.ppermute(pair, "batch", [(i, (i + 2 * k) % n_batch) for i in range(n_batch)])
        )
    sent, place = route(history, n_batch, n_item)
    per_peer = sent.shape[1]
    rim = jnp.mod(neighbours - (here - 1) * tiles_here, n_item * tiles_here)
    rim = jnp.broadcast_to(
        rim.reshape(n_batch, 1, row_tiles * slots), (n_batch, n_item, row_tiles * slots)
    ).reshape(peers, row_tiles * slots)
    got = exchange(jnp.concatenate([sent, rim], axis=1), everyone)
    wanted = got[:, :per_peer].reshape(-1, 128)
    tile_ids = lax.dynamic_index_in_dim(
        got[:, per_peer:].reshape(n_batch, n_item, row_tiles * slots), here, 1, keepdims=False
    ).reshape(-1)
    found = graph(tile_ids, mine.reshape(1), left, item_table, right, by_owner, swapped, arrived, wanted)
    rows = exchange(found.reshape(peers, per_peer, feat), everyone).reshape(-1, feat)
    pack_rows = peers * 24
    block_out, packed = attention(
        rows, place.reshape(-1), lengths, cotangent, position, norm_gain, in_weight,
        in_weight.T, out_weight, pack_rows, PART_TYPE,
    )
    parts = exchange(packed.reshape(peers, pack_rows // peers, 128), everyone)
    full = exchange(sum_spread(parts, SPREAD_TYPE), everyone).reshape(pack_rows, 128)
    full = full.astype(jnp.float32)
    slab = lambda a, b: jnp.concatenate(
        [full[feat * i : feat * i + feat] for i in range(a, b)], axis=1
    )
    gain_row = 10 * feat
    return (
        block_out,
        slab(0, 6),
        slab(6, 8),
        full[gain_row : gain_row + 2].reshape(feat),
        slab(8, 10),
    )


def solution(mesh):
    in_specs = (
        P("item", None),
        P("item", "batch"),
        P("item", "batch", None, None),
        P(("batch", "item"), None),
        P(("batch", "item")),
        P(),
        P(),
        P(),
        P(),
        P(("batch", "item"), None, None),
    )
    out_specs = (P(("batch", "item"), None, None), P(), P(), P(), P())
    return jax.shard_map(local, mesh=mesh, in_specs=in_specs, out_specs=out_specs, check_vma=False)
```
